512 devices in a mesh: seq: 64 (over z_lo, y, core), head: 8 (over x, z_hi).
Axes of the slice: x: 4, y: 4, z: 16 (z_hi: 2, z_lo: 8; z = z_hi * 8 + z_lo), core: 2. Of those that a mesh axis runs over, the one named last changes fastest.
Arguments:
- block_input: bfloat16 [18432, 3072], P('seq', 'head'), may hold values from -6 to 6
- mod_shift: float32 [3072], replicated, may hold values from -1.2 to 1.2
- mod_scale: float32 [3072], replicated, may hold values from -0.8 to 0.8
- history: float32 [16], replicated, may hold values from 3 to 6
- w_qkv: bfloat16 [3, 3072, 3072], P(None, 'seq', 'head')
- pattern: int32 [192, 12], P('seq'), may hold values from 0 to 191, as said below
- out_cotangent: bfloat16 [18432, 3072], P('seq', 'head'), may hold values from -6 to 6
Outputs:
- attn_out: bfloat16 [18432, 3072], P('seq', 'head')
- grad_qkv: bfloat16 [3, 18432, 3072], P(None, 'seq', 'head')
- new_history: float32 [16], replicated
The draws below stay inside these ranges and needn't reach their ends.
Inputs may be any that keep to these rules, and one draw needn't show every extreme that they name: `pattern`: row a lists 12 distinct tiles, the first being tile a itself; every listed tile lies in a's frame or the frame just before or after it, in a's tile row or the row just above or below it within the frame, and in a window of 3 tile columns around a's column, the window moved inward at a frame's side edges.
All inputs are finite; a program needn't handle non-finite values.
Results may differ from the reference program's by a relative error of at most 0.0096.
Values may be sent and summed in bfloat16 or wider, within the bound.
A program may use at most 64 MiB of HBM per device.

```python
import math
import jax
import jax.numpy as jnp
from jax import lax

D = 3072
HEADS = 24
HD = 128
TILE = 96
GRID_H = 8
GRID_W = 3
KB = 12
HIST = 16
FRAMES = 8
NTILES = 192
TOKENS = 18432
N_SEQ = 64


def draw_w_qkv(key, part):
    normal_part = jax.random.normal(key, (3, D, HEADS * HD), jnp.float32) * D ** (-0.5)
    return normal_part.astype(jnp.bfloat16)


def draw_pattern(key, part):
    tile_ids = jnp.arange(NTILES, dtype=jnp.int32)
    slab_ids = tile_ids // GRID_W
    tile_frame = slab_ids // GRID_H
    tile_row = slab_ids % GRID_H
    tile_col = tile_ids % GRID_W
    col_start = jnp.clip(tile_col - 1, 0, GRID_W - 3)
    step_frame = jnp.repeat(jnp.arange(3, dtype=jnp.int32) - 1, 9)
    step_row = jnp.tile(jnp.repeat(jnp.arange(3, dtype=jnp.int32) - 1, 3), 3)
    step_col = jnp.tile(jnp.arange(3, dtype=jnp.int32), 9)
    cand_frame = tile_frame[:, None] + step_frame[None, :]
    cand_row = tile_row[:, None] + step_row[None, :]
    in_range = (cand_frame >= 0) & (cand_frame < FRAMES) & (cand_row >= 0) & (cand_row < GRID_H)
    candidate = (cand_frame * GRID_H + cand_row) * GRID_W + col_start[:, None] + step_col[None, :]
    candidate = jnp.where(in_range, candidate, 0)
    random_score = jax.random.randint(key, (NTILES, 27), 0, 1 << 20, dtype=jnp.int32)
    rank_score = random_score * 64 + jnp.arange(27, dtype=jnp.int32)[None, :]
    rank_score = jnp.where(candidate == tile_ids[:, None], 1 << 28, jnp.where(in_range, rank_score, -1))
    chosen = lax.top_k(rank_score, KB)[1]
    return jnp.take_along_axis(candidate, chosen, axis=1).astype(jnp.int32)


def level_of(rng, dims, shards, least, top_value):
    level, own = 1.0, jax.random.fold_in(rng, 6)
    for dim, shards_of in shards:
        draws = jnp.exp(jax.random.uniform(jax.random.fold_in(own, dim), (shards_of,), jnp.float32, least / len(shards), top_value / len(shards)))
        level = level * jnp.repeat(draws, dims[dim] // shards_of).reshape([-1 if axis == dim else 1 for axis in range(len(dims))])
    return level


def noise(rng, extent, scale, limit, cuts=(), held_as=jnp.bfloat16):
    factor_of = level_of(rng, extent, cuts, -0.22, 0.18) if cuts else 1.0
    array = jax.random.normal(rng, extent, jnp.float32) * scale * factor_of
    return jnp.minimum(jnp.maximum(array, -limit), limit).astype(held_as)


def setup_inputs(seed: int = 0) -> dict:
    splits = jax.random.split(jax.random.key(seed), 8)
    return {
        "block_input": noise(splits[0], (TOKENS, D), 1.0, 6.0, ((0, 64), (1, 8))),
        "mod_shift": noise(splits[1], (D,), 0.3, 1.2, (), jnp.float32),
        "mod_scale": noise(splits[2], (D,), 0.2, 0.8, (), jnp.float32),
        "history": jnp.clip(jnp.exp(jax.random.uniform(splits[3], (HIST,), jnp.float32, math.log(3.0), math.log(6.0))), 3.0, 6.0),
        "w_qkv": draw_w_qkv(jax.random.fold_in(splits[7], 71), 0),
        "pattern": draw_pattern(jax.random.fold_in(splits[7], 71), 0),
        "out_cotangent": noise(splits[6], (TOKENS, HEADS * HD), 1.0, 6.0, ((0, 64), (1, 8))),
    }


LIMIT = 448.0
EPSILON = 1e-06

def modulate(full_rows, shift_vec, scale_vec):
    row_mean = lax.optimization_barrier(jnp.mean(full_rows, axis=1, keepdims=True))
    row_square = lax.optimization_barrier(jnp.mean(full_rows * full_rows, axis=1, keepdims=True))
    normed = (full_rows - row_mean) * lax.rsqrt(row_square - row_mean * row_mean + EPSILON)
    return normed * (1.0 + scale_vec) + shift_vec

def slot_ids(tile_ids, slab_index):
    offset = tile_ids // GRID_W - slab_index
    frame_step = (offset + 1) // GRID_H
    row_step = offset - frame_step * GRID_H
    slot_index = (frame_step + 1) * 3 + row_step + 1
    return (slot_index * GRID_W + tile_ids % GRID_W).astype(jnp.int32)

def reference(block_input, mod_shift, mod_scale, history, w_qkv, pattern, out_cotangent):
    peak_value = jnp.max(history)
    scale_up = LIMIT / peak_value
    scale_down = peak_value / LIMIT
    slab_tokens = TOKENS // N_SEQ
    feature_count = HEADS * HD

    def project(slab_rows):
        modulated = modulate(slab_rows.astype(jnp.float32), mod_shift, mod_scale)
        quantized = jnp.clip(modulated * scale_up, -LIMIT, LIMIT).astype(jnp.bfloat16)
        parts = [jnp.dot(quantized, w_qkv[which], preferred_element_type=jnp.float32) * scale_down for which in range(3)]
        return (jnp.stack(parts, axis=0).astype(jnp.bfloat16), jnp.max(jnp.abs(modulated)))
    qkv, slab_peaks = lax.map(project, block_input.reshape(N_SEQ, slab_tokens, D))
    abs_peak = jnp.max(slab_peaks)
    new_history = jnp.concatenate([abs_peak.reshape(1), history[:-1]])
    qkv = jnp.moveaxis(qkv, 1, 0).reshape(3, TOKENS, HEADS, HD)
    query_tiles = qkv[0].reshape(NTILES, TILE, HEADS, HD)
    key_tiles = qkv[1].reshape(NTILES, TILE, HEADS, HD)
    value_tiles = qkv[2].reshape(NTILES, TILE, HEADS, HD)
    grad_tiles = out_cotangent.reshape(NTILES, TILE, HEADS, HD)
    inv_root = HD ** (-0.5)
    window_ids = jnp.arange(9 * GRID_W, dtype=jnp.int32)

    def slab_step(slab_loop, state_tuple):
        out_all, query_grad_all, key_grad_all, value_grad_all = state_tuple
        slab_index = jnp.asarray(slab_loop).astype(jnp.int32)
        first_tile = (slab_index * GRID_W).astype(jnp.int32)
        key_index = lax.dynamic_slice_in_dim(pattern, first_tile, GRID_W, 0).reshape(-1)
        query_slab = lax.dynamic_slice_in_dim(query_tiles, first_tile, GRID_W, 0).astype(jnp.float32)
        grad_slab = lax.dynamic_slice_in_dim(grad_tiles, first_tile, GRID_W, 0).astype(jnp.float32)
        key_slab = jnp.take(key_tiles, key_index, axis=0).reshape(GRID_W, KB * TILE, HEADS, HD).astype(jnp.float32)
        value_slab = jnp.take(value_tiles, key_index, axis=0).reshape(GRID_W, KB * TILE, HEADS, HD).astype(jnp.float32)
        scores = jnp.einsum('aqhd,akhd->ahqk', query_slab, key_slab) * inv_root
        row_max = lax.optimization_barrier(jnp.max(scores, axis=3, keepdims=True))
        weights = jnp.exp(scores - row_max)
        softmax_w = weights / lax.optimization_barrier(jnp.sum(weights, axis=3, keepdims=True))
        softmax_low = lax.optimization_barrier(softmax_w.astype(jnp.bfloat16)).astype(jnp.float32)
        output = jnp.einsum('ahqk,akhd->aqhd', softmax_low, value_slab)
        grad_prob = jnp.einsum('aqhd,akhd->ahqk', grad_slab, value_slab)
        row_delta = lax.optimization_barrier(jnp.sum(softmax_w * grad_prob, axis=3, keepdims=True))
        grad_score = lax.optimization_barrier((softmax_w * (grad_prob - row_delta)).astype(jnp.bfloat16)).astype(jnp.float32)
        grad_query = jnp.einsum('ahqk,akhd->aqhd', grad_score, key_slab) * inv_root
        grad_key = jnp.einsum('ahqk,aqhd->akhd', grad_score, query_slab) * inv_root
        grad_value = jnp.einsum('ahqk,aqhd->akhd', softmax_low, grad_slab)
        local_ids = slot_ids(key_index, slab_index)
        onehot = (local_ids[:, None] == window_ids[None, :]).astype(jnp.float32)
        flat_key = grad_key.reshape(GRID_W * KB, TILE * HEADS * HD)
        flat_value = grad_value.reshape(GRID_W * KB, TILE * HEADS * HD)
        window_key = jnp.dot(onehot.T, flat_key, precision=lax.Precision.HIGHEST, preferred_element_type=jnp.float32)
        window_value = jnp.dot(onehot.T, flat_value, precision=lax.Precision.HIGHEST, preferred_element_type=jnp.float32)
        window_key = lax.optimization_barrier(window_key.astype(jnp.bfloat16)).astype(jnp.float32)
        window_value = lax.optimization_barrier(window_value.astype(jnp.bfloat16)).astype(jnp.float32)
        window_key = window_key.reshape(9, GRID_W, TILE, HEADS, HD)
        window_value = window_value.reshape(9, GRID_W, TILE, HEADS, HD)
        for slot_index in range(9):
            frame_step = slot_index // 3 - 1
            row_step = slot_index % 3 - 1
            target_tile = ((slab_index + frame_step * GRID_H + row_step) * GRID_W).astype(jnp.int32)
            current_key = lax.dynamic_slice_in_dim(key_grad_all, target_tile, GRID_W, 0)
            key_grad_all = lax.dynamic_update_slice_in_dim(key_grad_all, current_key + window_key[slot_index], target_tile, 0)
            current_value = lax.dynamic_slice_in_dim(value_grad_all, target_tile, GRID_W, 0)
            value_grad_all = lax.dynamic_update_slice_in_dim(value_grad_all, current_value + window_value[slot_index], target_tile, 0)
        out_all = lax.dynamic_update_slice_in_dim(out_all, output.astype(jnp.bfloat16), first_tile, 0)
        query_grad_all = lax.dynamic_update_slice_in_dim(query_grad_all, grad_query.astype(jnp.bfloat16), first_tile, 0)
        return (out_all, query_grad_all, key_grad_all, value_grad_all)
    initial = (jnp.zeros((NTILES, TILE, HEADS, HD), jnp.bfloat16), jnp.zeros((NTILES, TILE, HEADS, HD), jnp.bfloat16), jnp.zeros((NTILES, TILE, HEADS, HD), jnp.float32), jnp.zeros((NTILES, TILE, HEADS, HD), jnp.float32))
    out_all, query_grad_all, key_grad_all, value_grad_all = lax.fori_loop(0, N_SEQ, slab_step, initial)
    attn_out = out_all.reshape(TOKENS, feature_count)
    grad_qkv = jnp.stack([query_grad_all.reshape(TOKENS, feature_count).astype(jnp.float32), key_grad_all.reshape(TOKENS, feature_count), value_grad_all.reshape(TOKENS, feature_count)], axis=0).astype(jnp.bfloat16)
    return (attn_out, grad_qkv, new_history)
```

```python
import functools
import math

import jax
import jax.numpy as jnp
from jax import lax
from jax.experimental import pallas as pl
from jax.experimental.pallas import tpu as pltpu
from jax.sharding import PartitionSpec as P

HD = 128
TILE = 96
GRID_H = 8
NY = 4
NZ = 8
NX = 4
SLOTS = 9
KB = 12
LIMIT = 448.0
EPSILON = 1e-06
INV_ROOT = HD ** (-0.5)
EXP2_SCALE = INV_ROOT * math.log2(math.e)
MESH = pl.DeviceIdType.MESH


def seq_of(z_lo, y, core):
    return (z_lo * NY + y) * 2 + core


def place():
    seq = lax.axis_index("seq")
    head = lax.axis_index("head")
    return seq // (2 * NY), (seq // 2) % NY, seq % 2, head // 2, head % 2


def remote(src, dst, send, recv, device):
    return pltpu.make_async_remote_copy(
        src_ref=src,
        dst_ref=dst,
        send_sem=send,
        recv_sem=recv,
        device_id=device,
        device_id_type=MESH,
    )


def greet(devices):
    barrier = pltpu.get_barrier_semaphore()
    for device, valid in devices:
        if valid is None:
            pl.semaphore_signal(barrier, inc=1, device_id=device, device_id_type=MESH)
        else:

            @pl.when(valid)
            def _():
                pl.semaphore_signal(barrier, inc=1, device_id=device, device_id_type=MESH)

    count = jnp.int32(sum(valid is None for _, valid in devices))
    for _, valid in devices:
        if valid is not None:
            count = count + valid.astype(jnp.int32)
    pl.semaphore_wait(barrier, count)


def project_kernel(
    x_hbm, w_hbm, shift_ref, scale_ref, hist_ref,
    qkv_ref, peak_ref,
    xf, wf, rel, quant,
    local_sem, leg_s, leg_r, part_r, xs, xr, zs, zr, ys, yr, yos, yor, cs, cr,
):
    z_lo, y, core, x, z_hi = place()
    seq = seq_of(z_lo, y, core)
    head = x * 2 + z_hi
    rows = xf.shape[1]
    half = rows // 2
    z = z_hi * NZ + z_lo

    def ring_z(step):
        far = (z + step + 2 * NZ) % (2 * NZ)
        return (seq_of(far % NZ, y, core), x * 2 + far // NZ)

    def line_z(step):
        return (seq_of(z_lo + step, y, core), head)

    def ring_y(step):
        return (seq_of(z_lo, (y + step + NY) % NY, core), head)

    def ring_x(step):
        return (seq, ((x + step + NX) % NX) * 2 + z_hi)

    partner_core = (seq_of(z_lo, y, 1 - core), head)
    ahead, behind = ring_z(4), ring_z(-4)
    greet(
        [
            (ahead, None), (behind, None),
            (ring_x(1), None), (ring_x(-1), None),
            (ring_y(1), None), (ring_y(-1), None),
            (partner_core, None),
            (line_z(1), z_lo < NZ - 1), (line_z(-1), z_lo > 0),
        ]
    )
    own_x = pltpu.make_async_copy(x_hbm, xf.at[head], local_sem.at[0])
    own_x.start()
    own_w = pltpu.make_async_copy(w_hbm, wf.at[:, seq], local_sem.at[1])
    own_w.start()

    def part(ref, which):
        return ref.at[pl.ds(which * half, half)]

    leg_one = [
        remote(part(x_hbm, 0), rel.at[0], leg_s.at[0], leg_r.at[0], ahead),
        remote(part(x_hbm, 1), rel.at[1], leg_s.at[1], leg_r.at[1], behind),
    ]
    for copy in leg_one:
        copy.start()

    def z_copy(far_z, which, direction):
        slot = seq_of(far_z, y, core)
        side = 0 if direction > 0 else 1
        return remote(
            wf.at[which, slot], wf.at[which, slot], zs.at[side, far_z, which], zr.at[far_z, which],
            line_z(direction),
        )

    def y_copy(far_z, direction):
        slot = seq_of(far_z, y, core)
        side = 0 if direction > 0 else 1
        return remote(
            wf.at[:, slot], wf.at[:, slot], ys.at[side, far_z], yr.at[side, far_z], ring_y(direction)
        )

    def y_arrival(far_z, direction):
        slot = seq_of(far_z, (y - direction + NY) % NY, core)
        side = 0 if direction > 0 else 1
        return remote(
            wf.at[:, slot], wf.at[:, slot], ys.at[side, far_z], yr.at[side, far_z], ring_y(direction)
        )

    def y_forward(far_z, direction):
        slot = seq_of(far_z, (y - direction + NY) % NY, core)
        return remote(
            wf.at[:, slot], wf.at[:, slot], yos.at[far_z], yor.at[far_z], ring_y(direction)
        )

    def core_copy(far_z, far_y, order):
        slot = seq_of(far_z, far_y, core)
        return remote(
            wf.at[:, slot], wf.at[:, slot], cs.at[far_z, order], cr.at[far_z, order], partner_core
        )

    def have_shard(far_z):
        y_copy(far_z, 1).start()
        y_copy(far_z, -1).start()
        core_copy(far_z, y, 0).start()

    def y_step(far_z):
        for direction in (1, -1):
            far_y = (y - direction + NY) % NY
            y_arrival(far_z, direction).wait_recv()

            @pl.when(far_z % 2 == (0 if direction > 0 else 1))
            def _():
                y_forward(far_z, direction).start()

            core_copy(far_z, far_y, 1 if direction > 0 else 2).start()

    def opposite_step(far_z):
        far_y = (y + 2) % NY
        slot = seq_of(far_z, far_y, core)
        remote(
            wf.at[:, slot], wf.at[:, slot], yos.at[far_z], yor.at[far_z], ring_y(1)
        ).wait_recv()
        core_copy(far_z, far_y, 3).start()

    def inside(far_z):
        return (far_z >= 0) & (far_z < NZ)

    def z_step(step):
        for direction in (1, -1):
            far_z = z_lo - direction * step

            @pl.when(inside(far_z))
            def _():
                for which in range(3):
                    z_copy(far_z, which, direction).wait_recv()

                    @pl.when(inside(z_lo + direction))
                    def _():
                        z_copy(far_z, which, direction).start()

                have_shard(far_z)

    def each_side(step, act):
        for direction in (1, -1):
            far_z = z_lo - direction * step

            @pl.when(inside(far_z))
            def _():
                act(far_z)

    def x_copy(kind, which, direction):
        chunk = x * 2 + (z_hi if kind == 0 else 1 - z_hi)
        side = 0 if direction > 0 else 1
        ref = part(xf.at[chunk], which)
        return remote(ref, ref, xs.at[kind, which, side], xr.at[kind, which, side], ring_x(direction))

    def x_arrival(kind, which, direction):
        chunk = ((x - direction + NX) % NX) * 2 + (z_hi if kind == 0 else 1 - z_hi)
        side = 0 if direction > 0 else 1
        ref = part(xf.at[chunk], which)
        return remote(ref, ref, xs.at[kind, which, side], xr.at[kind, which, side], ring_x(direction))

    def x_forward(kind, which):
        direction = 1 if which == 0 else -1
        chunk = ((x - direction + NX) % NX) * 2 + (z_hi if kind == 0 else 1 - z_hi)
        ref = part(xf.at[chunk], which)
        return remote(ref, ref, xs.at[kind, which, 2], xr.at[kind, which, 2], ring_x(direction))

    def x_opposite(kind, which):
        direction = 1 if which == 0 else -1
        chunk = ((x + 2) % NX) * 2 + (z_hi if kind == 0 else 1 - z_hi)
        ref = part(xf.at[chunk], which)
        return remote(ref, ref, xs.at[kind, which, 2], xr.at[kind, which, 2], ring_x(direction))

    own_w.wait()
    for which in range(3):
        for direction in (1, -1):

            @pl.when(inside(z_lo + direction))
            def _():
                z_copy(z_lo, which, direction).start()

    own_x.wait()
    for which in (0, 1):
        for direction in (1, -1):
            x_copy(0, which, direction).start()
    have_shard(z_lo)

    z_step(1)
    far_chunk = x * 2 + (1 - z_hi)
    leg_two = []
    for which, to in ((0, ahead), (1, behind)):
        leg_one[which].wait_recv()
        source = (z - 4 + 2 * NZ) % (2 * NZ) if which == 0 else (z + 4) % (2 * NZ)
        chunk = x * 2 + source // NZ
        copy = remote(
            rel.at[which], part(xf.at[chunk], which), leg_s.at[2 + which], part_r.at[which], to
        )
        copy.start()
        leg_two.append(copy)
    y_step(z_lo)
    z_step(2)
    each_side(1, y_step)
    opposite_step(z_lo)
    for which in (0, 1):
        x_arrival(0, which, 1).wait_recv()
        x_arrival(0, which, -1).wait_recv()
        x_forward(0, which).start()

    def step_loop(step, _):
        z_step(step)
        each_side(step - 1, y_step)
        each_side(step - 2, opposite_step)
        return 0

    lax.fori_loop(3, 5, step_loop, 0)
    for which in (0, 1):
        ref = part(xf.at[far_chunk], which)
        remote(ref, ref, leg_s.at[2 + which], part_r.at[which], ahead).wait_recv()
        for direction in (1, -1):
            x_copy(1, which, direction).start()
    lax.fori_loop(5, 7, step_loop, 0)
    for which in (0, 1):
        x_arrival(1, which, 1).wait_recv()
        x_arrival(1, which, -1).wait_recv()
        x_forward(1, which).start()
    lax.fori_loop(7, 8, step_loop, 0)
    each_side(7, y_step)
    each_side(6, opposite_step)
    for kind in (0, 1):
        for which in (0, 1):
            x_opposite(kind, which).wait_recv()

    peak = jnp.max(hist_ref[...], axis=1, keepdims=True)
    scale_up = LIMIT / peak
    scale_down = peak / LIMIT
    chunks = xf.shape[0]
    width = xf.shape[2]
    features = chunks * width
    block = 32

    def norm_rows(index, largest):
        at = pl.ds(pl.multiple_of(index * block, block), block)
        total = jnp.zeros((block, width), jnp.float32)
        square = jnp.zeros((block, width), jnp.float32)
        for chunk in range(chunks):
            value = xf[chunk, at, :].astype(jnp.float32)
            total = total + value
            square = square + value * value
        mean = jnp.sum(total, axis=1, keepdims=True) * (1.0 / features)
        mean_square = jnp.sum(square, axis=1, keepdims=True) * (1.0 / features)
        inverse = lax.rsqrt(mean_square - mean * mean + EPSILON)
        for chunk in range(chunks):
            value = xf[chunk, at, :].astype(jnp.float32)
            columns = pl.ds(chunk * width, width)
            modulated = (value - mean) * inverse * (1.0 + scale_ref[:, columns]) + shift_ref[:, columns]
            largest = jnp.maximum(largest, jnp.max(jnp.abs(modulated), axis=0, keepdims=True))
            quant[at, columns] = jnp.clip(modulated * scale_up, -LIMIT, LIMIT).astype(jnp.bfloat16)
        return largest

    largest = lax.fori_loop(0, rows // block, norm_rows, jnp.zeros((1, width), jnp.float32))
    peak_ref[...] = jnp.broadcast_to(jnp.max(largest, axis=1, keepdims=True), peak_ref.shape)

    each_side(7, opposite_step)
    def core_arrivals(far_z, _):
        for order in range(4):
            slot = seq_of(far_z, 0, 1 - core)
            remote(
                wf.at[:, slot], wf.at[:, slot], cs.at[far_z, order], cr.at[far_z, order], partner_core
            ).wait_recv()
        return 0

    lax.fori_loop(0, NZ, core_arrivals, 0)
    depth = wf.shape[1] * wf.shape[2]

    def multiply(which, _):
        weight = wf[which].reshape(depth, width)
        product = jnp.dot(quant[...], weight, preferred_element_type=jnp.float32) * scale_down
        for head_here in range(width // HD):
            qkv_ref[which, head_here] = product[:, head_here * HD : (head_here + 1) * HD].astype(
                jnp.bfloat16
            )
        return 0

    lax.fori_loop(0, 3, multiply, 0)

    for copy in leg_one + leg_two:
        copy.wait_send()
    for kind in (0, 1):
        for which in (0, 1):
            x_copy(kind, which, 1).wait_send()
            x_copy(kind, which, -1).wait_send()
            x_forward(kind, which).wait_send()

    def drain(far_z, _):
        for direction in (1, -1):
            y_copy(far_z, direction).wait_send()

            @pl.when(inside(z_lo + direction) & ((z_lo - far_z) * direction >= 0))
            def _():
                for which in range(3):
                    z_copy(far_z, which, direction).wait_send()

        y_forward(far_z, 1).wait_send()
        for order in range(4):
            core_copy(far_z, y, order).wait_send()
        return 0

    lax.fori_loop(0, NZ, drain, 0)


def project(block_input, mod_shift, mod_scale, history, w_qkv):
    rows, width = block_input.shape
    three, depth, _ = w_qkv.shape
    seqs = lax.axis_size("seq")
    heads = lax.axis_size("head")
    dma = pltpu.SemaphoreType.DMA
    any_space = pl.BlockSpec(memory_space=pl.ANY)
    vmem = pl.BlockSpec(memory_space=pltpu.VMEM)
    return pl.pallas_call(
        project_kernel,
        out_shape=(
            jax.ShapeDtypeStruct((three, width // HD, rows, HD), jnp.bfloat16),
            jax.ShapeDtypeStruct((8, 128), jnp.float32),
        ),
        in_specs=[any_space, any_space, vmem, vmem, vmem],
        out_specs=(vmem, vmem),
        scratch_shapes=[
            pltpu.VMEM((heads, rows, width), jnp.bfloat16),
            pltpu.VMEM((three, seqs, depth, width), jnp.bfloat16),
            pltpu.VMEM((2, rows // 2, width), jnp.bfloat16),
            pltpu.VMEM((rows, heads * width), jnp.bfloat16),
            dma((2,)), dma((4,)), dma((2,)), dma((2,)),
            dma((2, 2, 3)), dma((2, 2, 3)),
            dma((2, NZ, 3)), dma((NZ, 3)),
            dma((2, NZ)), dma((2, NZ)),
            dma((NZ,)), dma((NZ,)),
            dma((NZ, 4)), dma((NZ, 4)),
        ],
        compiler_params=pltpu.CompilerParams(collective_id=0, has_side_effects=True),
        name="gather_project",
    )(block_input, w_qkv, mod_shift.reshape(1, -1), mod_scale.reshape(1, -1), history.reshape(1, -1))


def row_device(z_lo, row, head):
    return (z_lo * GRID_H + row, head)


def halo_kernel(qkv_hbm, peak_hbm, win_hbm, peak_ref, near, far, zs, zr, rs, rr, ms, mr, local_sem):
    z_lo, y, core, x, z_hi = place()
    head = x * 2 + z_hi
    row = y * 2 + core
    up, down = row_device(z_lo, row - 1, head), row_device(z_lo, row + 1, head)
    before, after = row_device(z_lo - 1, row, head), row_device(z_lo + 1, row, head)
    has_up, has_down = row > 0, row < GRID_H - 1
    has_before, has_after = z_lo > 0, z_lo < NZ - 1
    peers_row = [row_device(z_lo, (row + k) % GRID_H, head) for k in range(1, GRID_H)]
    peers_z = [row_device((z_lo + k) % NZ, row, head) for k in range(1, NZ)]
    greet([(d, None) for d in peers_row + peers_z])

    own_peak = pltpu.make_async_copy(peak_hbm, near.at[row], local_sem.at[0])
    own_peak.start()

    def max_near(k):
        return remote(
            peak_hbm, near.at[row], ms.at[0, k - 1], mr.at[0, k - 1], peers_row[k - 1]
        )

    def max_far(k):
        return remote(near, far.at[z_lo], ms.at[1, k - 1], mr.at[1, k - 1], peers_z[k - 1])

    frame_slot = (1, 0, 2)

    def z_copy(part, side):
        slot = 2 if side == 0 else 0
        target, at = (before, 1) if side == 0 else (after, 0)
        del slot
        frame = 2 if side == 0 else 0
        return remote(
            qkv_hbm.at[1 + part], win_hbm.at[frame * 3 + 1, part], zs.at[side, part], zr.at[side, part],
            target,
        )

    for part in (0, 1):
        for side, valid in ((0, has_before), (1, has_after)):

            @pl.when(valid)
            def _():
                z_copy(part, side).start()

    def row_copy(frame, part, side):
        target = up if side == 0 else down
        slot = frame * 3 + (2 if side == 0 else 0)
        source = qkv_hbm.at[1 + part] if frame == 1 else win_hbm.at[frame * 3 + 1, part]
        return remote(
            source, win_hbm.at[slot, part], rs.at[frame, part, side], rr.at[frame, part, side], target
        )

    def rows_out(frame, part):
        for side, valid in ((0, has_up), (1, has_down)):

            @pl.when(valid)
            def _():
                row_copy(frame, part, side).start()

    for k in range(1, GRID_H):
        max_near(k).start()
    for part in (0, 1):
        rows_out(1, part)
    own_peak.wait()
    for k in range(1, GRID_H):
        max_near(k).wait_recv()
    for k in range(1, NZ):
        max_far(k).start()
    arrivals = ((2, 0, has_after), (0, 1, has_before))
    for part in (0, 1):
        for frame, side, valid in arrivals:

            @pl.when(valid)
            def _():
                z_copy(part, side).wait_recv()
                rows_out(frame, part)

    for k in range(1, NZ):
        max_far(k).wait_recv()
    own_far = pltpu.make_async_copy(near, far.at[z_lo], local_sem.at[1])
    own_far.start()
    own_far.wait()
    top = jnp.max(jnp.max(far[...], axis=0), axis=0)
    peak_ref[...] = top

    frames = ((1, None), (2, has_after), (0, has_before))
    for frame, valid_frame in frames:
        for side, valid in ((0, has_down), (1, has_up)):
            ok = valid if valid_frame is None else valid & valid_frame

            @pl.when(ok)
            def _():
                for part in (0, 1):
                    row_copy(frame, part, side).wait_recv()

        for side, valid in ((0, has_up), (1, has_down)):
            ok = valid if valid_frame is None else valid & valid_frame

            @pl.when(ok)
            def _():
                for part in (0, 1):
                    row_copy(frame, part, side).wait_send()

    for part in (0, 1):
        for side, valid in ((0, has_before), (1, has_after)):

            @pl.when(valid)
            def _():
                z_copy(part, side).wait_send()

    for k in range(1, GRID_H):
        max_near(k).wait_send()
    for k in range(1, NZ):
        max_far(k).wait_send()


def halo(qkv, peak):
    _, heads, rows, _ = qkv.shape
    dma = pltpu.SemaphoreType.DMA
    any_space = pl.BlockSpec(memory_space=pl.ANY)
    return pl.pallas_call(
        halo_kernel,
        out_shape=(
            jax.ShapeDtypeStruct((SLOTS, 2, heads, rows, HD), jnp.bfloat16),
            jax.ShapeDtypeStruct((8, 128), jnp.float32),
        ),
        in_specs=[any_space, any_space],
        out_specs=(any_space, pl.BlockSpec(memory_space=pltpu.VMEM)),
        scratch_shapes=[
            pltpu.VMEM((GRID_H, 8, 128), jnp.float32),
            pltpu.VMEM((NZ, GRID_H, 8, 128), jnp.float32),
            dma((2, 2)), dma((2, 2)),
            dma((3, 2, 2)), dma((3, 2, 2)),
            dma((2, 7)), dma((2, 7)),
            dma((2,)),
        ],
        compiler_params=pltpu.CompilerParams(collective_id=1, has_side_effects=True),
        name="halo",
    )(qkv, peak)


def attend_kernel(ids_ref, qkv_hbm, win_hbm, grad_ref, out_ref, gq_ref, part_ref, win, query, acc, sems):
    heads = query.shape[0]
    copies = [pltpu.make_async_copy(qkv_hbm.at[0], query, sems.at[0])]
    for slot in range(SLOTS):
        source = qkv_hbm.at[pl.ds(1, 2)] if slot == 4 else win_hbm.at[slot]
        copies.append(pltpu.make_async_copy(source, win.at[slot], sems.at[1 + slot]))
    for copy in copies:
        copy.start()
    for copy in copies:
        copy.wait()
    tiles = query.shape[1]

    def one_head(head, _):
        columns = pl.ds(pl.multiple_of(head * HD, HD), HD)
        acc[...] = jnp.zeros_like(acc)

        def one_tile(tile, _):
            listed = [ids_ref[tile, slot] for slot in range(KB)]
            q = query[head, tile]
            g = grad_ref[tile, :, columns]
            keys = jnp.concatenate([win[i // 3, 0, head, i % 3] for i in listed], axis=0)
            values = jnp.concatenate([win[i // 3, 1, head, i % 3] for i in listed], axis=0)
            scores = lax.dot_general(
                q, keys, (((1,), (1,)), ((), ())), preferred_element_type=jnp.float32
            )
            top = jnp.max(scores, axis=1, keepdims=True)
            weights = jnp.exp2((scores - top) * EXP2_SCALE)
            prob = weights * (1.0 / jnp.sum(weights, axis=1, keepdims=True))
            low = prob.astype(jnp.bfloat16)
            out = jnp.dot(low, values, preferred_element_type=jnp.float32)
            out_ref[tile, :, columns] = out.astype(jnp.bfloat16)
            gprob = lax.dot_general(
                g, values, (((1,), (1,)), ((), ())), preferred_element_type=jnp.float32
            )
            delta = jnp.sum(g.astype(jnp.float32) * out, axis=1, keepdims=True)
            gscore = (prob * (gprob - delta)).astype(jnp.bfloat16)
            gq = jnp.dot(gscore, keys, preferred_element_type=jnp.float32) * INV_ROOT
            gq_ref[tile, :, columns] = gq.astype(jnp.bfloat16)
            gk = lax.dot_general(
                gscore, q, (((0,), (0,)), ((), ())), preferred_element_type=jnp.float32
            )
            gv = lax.dot_general(
                low, g, (((0,), (0,)), ((), ())), preferred_element_type=jnp.float32
            )
            for slot, i in enumerate(listed):
                span = slice(slot * TILE, (slot + 1) * TILE)
                acc[0, i] += gk[span]
                acc[1, i] += gv[span]
            return 0

        lax.fori_loop(0, tiles, one_tile, 0)

        def write(frame, _):
            for row in range(3):
                for tile in range(3):
                    at = (frame * 3 + row) * 3 + tile
                    part_ref[row, frame, 0, head, tile] = (acc[0, at] * INV_ROOT).astype(jnp.bfloat16)
                    part_ref[row, frame, 1, head, tile] = acc[1, at].astype(jnp.bfloat16)
            return 0

        lax.fori_loop(0, 3, write, 0)
        return 0

    lax.fori_loop(0, heads, one_head, 0)


def attend(ids, qkv, win, out_cotangent):
    _, heads, rows, _ = qkv.shape
    tiles = rows // TILE
    width = heads * HD
    any_space = pl.BlockSpec(memory_space=pl.ANY)
    vmem = pl.BlockSpec(memory_space=pltpu.VMEM)
    return pl.pallas_call(
        attend_kernel,
        out_shape=(
            jax.ShapeDtypeStruct((tiles, TILE, width), jnp.bfloat16),
            jax.ShapeDtypeStruct((tiles, TILE, width), jnp.bfloat16),
            jax.ShapeDtypeStruct((3, 3, 2, heads, tiles, TILE, HD), jnp.bfloat16),
        ),
        in_specs=[pl.BlockSpec(memory_space=pltpu.SMEM), any_space, any_space, vmem],
        out_specs=(vmem, vmem, vmem),
        scratch_shapes=[
            pltpu.VMEM((SLOTS, 2, heads, tiles, TILE, HD), jnp.bfloat16),
            pltpu.VMEM((heads, tiles, TILE, HD), jnp.bfloat16),
            pltpu.VMEM((2, SLOTS * tiles, TILE, HD), jnp.float32),
            pltpu.SemaphoreType.DMA((1 + SLOTS,)),
        ],
        name="attend",
    )(
        ids,
        qkv.reshape(3, heads, tiles, TILE, HD),
        win.reshape(SLOTS, 2, heads, tiles, TILE, HD),
        out_cotangent.reshape(tiles, TILE, width),
    )


def return_kernel(part_hbm, out_ref, own, rows_in, zout, zin, local_sem, rs, rr, zs, zr):
    z_lo, y, core, x, z_hi = place()
    head = x * 2 + z_hi
    row = y * 2 + core
    up, down = row_device(z_lo, row - 1, head), row_device(z_lo, row + 1, head)
    before, after = row_device(z_lo - 1, row, head), row_device(z_lo + 1, row, head)
    has_up, has_down = row > 0, row < GRID_H - 1
    has_before, has_after = z_lo > 0, z_lo < NZ - 1
    greet([(up, has_up), (down, has_down), (before, has_before), (after, has_after)])
    mine = pltpu.make_async_copy(part_hbm.at[1], own, local_sem)
    mine.start()
    frames = ((0, has_before), (2, has_after), (1, None))

    def row_copy(frame, part, side):
        target = up if side == 0 else down
        step = 0 if side == 0 else 2
        return remote(
            part_hbm.at[step, frame, part], rows_in.at[side, frame, part],
            rs.at[frame, part, side], rr.at[frame, part, side], target,
        )

    def both(a, b):
        return a if b is None else a & b

    for part in (0, 1):
        for frame, valid_frame in frames:
            for side, valid in ((0, has_up), (1, has_down)):

                @pl.when(both(valid, valid_frame))
                def _():
                    row_copy(frame, part, side).start()

    @pl.when(jnp.logical_not(has_down))
    def _():
        rows_in[0] = jnp.zeros(rows_in.shape[1:], rows_in.dtype)

    @pl.when(jnp.logical_not(has_up))
    def _():
        rows_in[1] = jnp.zeros(rows_in.shape[1:], rows_in.dtype)

    @pl.when(jnp.logical_not(has_after))
    def _():
        zin[0] = jnp.zeros(zin.shape[1:], zin.dtype)

    @pl.when(jnp.logical_not(has_before))
    def _():
        zin[1] = jnp.zeros(zin.shape[1:], zin.dtype)

    mine.wait()

    def z_copy(part, side):
        target = before if side == 0 else after
        return remote(
            zout.at[side, part], zin.at[side, part], zs.at[side, part], zr.at[side, part], target
        )

    def arrived(frame, part, valid_frame):
        for side, valid in ((0, has_down), (1, has_up)):

            @pl.when(both(valid, valid_frame))
            def _():
                row_copy(frame, part, side).wait_recv()

    def total(frame, part, head_here):
        return (
            own[frame, part, head_here].astype(jnp.float32)
            + rows_in[0, frame, part, head_here].astype(jnp.float32)
            + rows_in[1, frame, part, head_here].astype(jnp.float32)
        )

    heads = own.shape[2]
    for part in (0, 1):
        for frame, side, valid_frame in ((0, 0, has_before), (2, 1, has_after)):
            arrived(frame, part, valid_frame)

            @pl.when(valid_frame)
            def _():
                for head_here in range(heads):
                    zout[side, part, head_here] = total(frame, part, head_here).astype(jnp.bfloat16)
                z_copy(part, side).start()

    for part in (0, 1):
        arrived(1, part, None)
        for side, valid in ((0, has_after), (1, has_before)):

            @pl.when(valid)
            def _():
                z_copy(part, side).wait_recv()

        for head_here in range(heads):
            result = (
                total(1, part, head_here)
                + zin[0, part, head_here].astype(jnp.float32)
                + zin[1, part, head_here].astype(jnp.float32)
            )
            out_ref[part, :, head_here * HD : (head_here + 1) * HD] = result.astype(jnp.bfloat16)

    for part in (0, 1):
        for frame, valid_frame in frames:
            for side, valid in ((0, has_up), (1, has_down)):

                @pl.when(both(valid, valid_frame))
                def _():
                    row_copy(frame, part, side).wait_send()

        for side, valid in ((0, has_before), (1, has_after)):

            @pl.when(valid)
            def _():
                z_copy(part, side).wait_send()


def give_back(parts):
    _, _, _, heads, rows, _ = parts.shape
    dma = pltpu.SemaphoreType.DMA
    half = (2, heads, rows, HD)
    return pl.pallas_call(
        return_kernel,
        out_shape=jax.ShapeDtypeStruct((2, rows, heads * HD), jnp.bfloat16),
        in_specs=[pl.BlockSpec(memory_space=pl.ANY)],
        out_specs=pl.BlockSpec(memory_space=pltpu.VMEM),
        scratch_shapes=[
            pltpu.VMEM((3,) + half, jnp.bfloat16),
            pltpu.VMEM((2, 3) + half, jnp.bfloat16),
            pltpu.VMEM((2,) + half, jnp.bfloat16),
            pltpu.VMEM((2,) + half, jnp.bfloat16),
            dma(()),
            dma((3, 2, 2)), dma((3, 2, 2)),
            dma((2, 2)), dma((2, 2)),
        ],
        compiler_params=pltpu.CompilerParams(collective_id=2, has_side_effects=True),
        name="give_back",
    )(parts)


def local(block_input, mod_shift, mod_scale, history, w_qkv, pattern, out_cotangent):
    rows, width = block_input.shape
    tiles = rows // TILE
    heads = width // HD
    qkv, peak = project(block_input, mod_shift, mod_scale, history, w_qkv)
    win, peak_all = halo(qkv, peak)
    tile_offset = pattern // tiles - lax.axis_index("seq")
    frame_of = (tile_offset + 1) // GRID_H
    slot_of = (frame_of + 1) * 3 + tile_offset - frame_of * GRID_H + 1
    ids = slot_of * tiles + pattern % tiles
    attn_out, grad_query, parts = attend(ids, qkv, win, out_cotangent)
    grad_kv = give_back(parts.reshape(3, 3, 2, heads, rows, HD))
    grad_qkv = jnp.concatenate([grad_query.reshape(1, rows, width), grad_kv], axis=0)
    new_history = jnp.concatenate([peak_all[0, :1], history[:-1]])
    return (attn_out.reshape(rows, width), grad_qkv, new_history)


def solution(mesh):
    placed = (
        P("seq", "head"),
        P(),
        P(),
        P(),
        P(None, "seq", "head"),
        P("seq", None),
        P("seq", "head"),
    )
    return jax.shard_map(
        local,
        mesh=mesh,
        in_specs=placed,
        out_specs=(P("seq", "head"), P(None, "seq", "head"), P()),
        check_vma=False,
    )
```

```python
import functools
import math

import jax
import jax.numpy as jnp
from jax import lax
from jax.experimental import pallas as pl
from jax.experimental.pallas import tpu as pltpu
from jax.sharding import PartitionSpec as P

HD = 128
TILE = 96
GRID_H = 8
NY = 4
NZ = 8
NX = 4
SLOTS = 9
KB = 12
LIMIT = 448.0
EPSILON = 1e-06
INV_ROOT = HD ** (-0.5)
EXP2_SCALE = INV_ROOT * math.log2(math.e)
MESH = pl.DeviceIdType.MESH


def seq_of(z_lo, y, core):
    return (z_lo * NY + y) * 2 + core


def place():
    seq = lax.axis_index("seq")
    head = lax.axis_index("head")
    return seq // (2 * NY), (seq // 2) % NY, seq % 2, head // 2, head % 2


def remote(src, dst, send, recv, device):
    return pltpu.make_async_remote_copy(
        src_ref=src,
        dst_ref=dst,
        send_sem=send,
        recv_sem=recv,
        device_id=device,
        device_id_type=MESH,
    )


def greet(devices):
    barrier = pltpu.get_barrier_semaphore()
    for device, valid in devices:
        if valid is None:
            pl.semaphore_signal(barrier, inc=1, device_id=device, device_id_type=MESH)
        else:

            @pl.when(valid)
            def _():
                pl.semaphore_signal(barrier, inc=1, device_id=device, device_id_type=MESH)

    count = jnp.int32(sum(valid is None for _, valid in devices))
    for _, valid in devices:
        if valid is not None:
            count = count + valid.astype(jnp.int32)
    pl.semaphore_wait(barrier, count)


def project_kernel(
    x_hbm, w_hbm, shift_ref, scale_ref, hist_ref,
    qkv_ref, peak_ref,
    xf, wf, rel, quant,
    local_sem, leg_s, leg_r, part_r, xs, xr, zs, zr, ys, yr, yos, yor, cs, cr,
):
    z_lo, y, core, x, z_hi = place()
    seq = seq_of(z_lo, y, core)
    head = x * 2 + z_hi
    rows = xf.shape[1]
    half = rows // 2
    z = z_hi * NZ + z_lo

    def ring_z(step):
        far = (z + step + 2 * NZ) % (2 * NZ)
        return (seq_of(far % NZ, y, core), x * 2 + far // NZ)

    def line_z(step):
        return (seq_of(z_lo + step, y, core), head)

    def ring_y(step):
        return (seq_of(z_lo, (y + step + NY) % NY, core), head)

    def ring_x(step):
        return (seq, ((x + step + NX) % NX) * 2 + z_hi)

    partner_core = (seq_of(z_lo, y, 1 - core), head)
    ahead, behind = ring_z(4), ring_z(-4)
    greet(
        [
            (ahead, None), (behind, None),
            (ring_x(1), None), (ring_x(-1), None),
            (ring_y(1), None), (ring_y(-1), None),
            (partner_core, None),
            (line_z(1), z_lo < NZ - 1), (line_z(-1), z_lo > 0),
        ]
    )
    own_x = pltpu.make_async_copy(x_hbm, xf.at[head], local_sem.at[0])
    own_x.start()
    own_w = pltpu.make_async_copy(w_hbm, wf.at[:, seq], local_sem.at[1])
    own_w.start()

    def part(ref, which):
        return ref.at[pl.ds(which * half, half)]

    leg_one = [
        remote(part(x_hbm, 0), rel.at[0], leg_s.at[0], leg_r.at[0], ahead),
        remote(part(x_hbm, 1), rel.at[1], leg_s.at[1], leg_r.at[1], behind),
    ]
    for copy in leg_one:
        copy.start()

    def z_copy(far_z, which, direction):
        slot = seq_of(far_z, y, core)
        side = 0 if direction > 0 else 1
        return remote(
            wf.at[which, slot], wf.at[which, slot], zs.at[side, far_z, which], zr.at[far_z, which],
            line_z(direction),
        )

    def y_copy(far_z, direction):
        slot = seq_of(far_z, y, core)
        side = 0 if direction > 0 else 1
        return remote(
            wf.at[:, slot], wf.at[:, slot], ys.at[side, far_z], yr.at[side, far_z], ring_y(direction)
        )

    def y_arrival(far_z, direction):
        slot = seq_of(far_z, (y - direction + NY) % NY, core)
        side = 0 if direction > 0 else 1
        return remote(
            wf.at[:, slot], wf.at[:, slot], ys.at[side, far_z], yr.at[side, far_z], ring_y(direction)
        )

    def y_forward(far_z, direction):
        slot = seq_of(far_z, (y - direction + NY) % NY, core)
        return remote(
            wf.at[:, slot], wf.at[:, slot], yos.at[far_z], yor.at[far_z], ring_y(direction)
        )

    def core_copy(far_z, far_y, order):
        slot = seq_of(far_z, far_y, core)
        return remote(
            wf.at[:, slot], wf.at[:, slot], cs.at[far_z, order], cr.at[far_z, order], partner_core
        )

    def have_shard(far_z):
        y_copy(far_z, 1).start()
        y_copy(far_z, -1).start()
        core_copy(far_z, y, 0).start()

    def y_step(far_z):
        for direction in (1, -1):
            far_y = (y - direction + NY) % NY
            y_arrival(far_z, direction).wait_recv()

            @pl.when(far_z % 2 == (0 if direction > 0 else 1))
            def _():
                y_forward(far_z, direction).start()

            core_copy(far_z, far_y, 1 if direction > 0 else 2).start()

    def opposite_step(far_z):
        far_y = (y + 2) % NY
        slot = seq_of(far_z, far_y, core)
        remote(
            wf.at[:, slot], wf.at[:, slot], yos.at[far_z], yor.at[far_z], ring_y(1)
        ).wait_recv()
        core_copy(far_z, far_y, 3).start()

    def inside(far_z):
        return (far_z >= 0) & (far_z < NZ)

    def z_step(step):
        for direction in (1, -1):
            far_z = z_lo - direction * step

            @pl.when(inside(far_z))
            def _():
                for which in range(3):
                    z_copy(far_z, which, direction).wait_recv()

                    @pl.when(inside(z_lo + direction))
                    def _():
                        z_copy(far_z, which, direction).start()

                have_shard(far_z)

    def each_side(step, act):
        for direction in (1, -1):
            far_z = z_lo - direction * step

            @pl.when(inside(far_z))
            def _():
                act(far_z)

    def x_copy(kind, which, direction):
        chunk = x * 2 + (z_hi if kind == 0 else 1 - z_hi)
        side = 0 if direction > 0 else 1
        ref = part(xf.at[chunk], which)
        return remote(ref, ref, xs.at[kind, which, side], xr.at[kind, which, side], ring_x(direction))

    def x_arrival(kind, which, direction):
        chunk = ((x - direction + NX) % NX) * 2 + (z_hi if kind == 0 else 1 - z_hi)
        side = 0 if direction > 0 else 1
        ref = part(xf.at[chunk], which)
        return remote(ref, ref, xs.at[kind, which, side], xr.at[kind, which, side], ring_x(direction))

    def x_forward(kind, which):
        direction = 1 if which == 0 else -1
        chunk = ((x - direction + NX) % NX) * 2 + (z_hi if kind == 0 else 1 - z_hi)
        ref = part(xf.at[chunk], which)
        return remote(ref, ref, xs.at[kind, which, 2], xr.at[kind, which, 2], ring_x(direction))

    def x_opposite(kind, which):
        direction = 1 if which == 0 else -1
        chunk = ((x + 2) % NX) * 2 + (z_hi if kind == 0 else 1 - z_hi)
        ref = part(xf.at[chunk], which)
        return remote(ref, ref, xs.at[kind, which, 2], xr.at[kind, which, 2], ring_x(direction))

    own_w.wait()
    for which in range(3):
        for direction in (1, -1):

            @pl.when(inside(z_lo + direction))
            def _():
                z_copy(z_lo, which, direction).start()

    own_x.wait()
    for which in (0, 1):
        for direction in (1, -1):
            x_copy(0, which, direction).start()
    have_shard(z_lo)

    z_step(1)
    far_chunk = x * 2 + (1 - z_hi)
    leg_two = []
    for which, to in ((0, ahead), (1, behind)):
        leg_one[which].wait_recv()
        source = (z - 4 + 2 * NZ) % (2 * NZ) if which == 0 else (z + 4) % (2 * NZ)
        chunk = x * 2 + source // NZ
        copy = remote(
            rel.at[which], part(xf.at[chunk], which), leg_s.at[2 + which], part_r.at[which], to
        )
        copy.start()
        leg_two.append(copy)
    y_step(z_lo)
    z_step(2)
    each_side(1, y_step)
    opposite_step(z_lo)
    for which in (0, 1):
        x_arrival(0, which, 1).wait_recv()
        x_arrival(0, which, -1).wait_recv()
        x_forward(0, which).start()

    def step_loop(step, _):
        z_step(step)
        each_side(step - 1, y_step)
        each_side(step - 2, opposite_step)
        return 0

    lax.fori_loop(3, 5, step_loop, 0)
    for which in (0, 1):
        ref = part(xf.at[far_chunk], which)
        remote(ref, ref, leg_s.at[2 + which], part_r.at[which], ahead).wait_recv()
        for direction in (1, -1):
            x_copy(1, which, direction).start()
    lax.fori_loop(5, 7, step_loop, 0)
    for which in (0, 1):
        x_arrival(1, which, 1).wait_recv()
        x_arrival(1, which, -1).wait_recv()
        x_forward(1, which).start()
    lax.fori_loop(7, 8, step_loop, 0)
    each_side(7, y_step)
    each_side(6, opposite_step)
    for kind in (0, 1):
        for which in (0, 1):
            x_opposite(kind, which).wait_recv()

    peak = jnp.max(hist_ref[...], axis=1, keepdims=True)
    scale_up = LIMIT / peak
    scale_down = peak / LIMIT
    chunks = xf.shape[0]
    width = xf.shape[2]
    features = chunks * width
    block = 32

    def norm_rows(index, largest):
        at = pl.ds(pl.multiple_of(index * block, block), block)
        total = jnp.zeros((block, width), jnp.float32)
        square = jnp.zeros((block, width), jnp.float32)
        for chunk in range(chunks):
            value = xf[chunk, at, :].astype(jnp.float32)
            total = total + value
            square = square + value * value
        mean = jnp.sum(total, axis=1, keepdims=True) * (1.0 / features)
        mean_square = jnp.sum(square, axis=1, keepdims=True) * (1.0 / features)
        inverse = lax.rsqrt(mean_square - mean * mean + EPSILON)
        for chunk in range(chunks):
            value = xf[chunk, at, :].astype(jnp.float32)
            columns = pl.ds(chunk * width, width)
            modulated = (value - mean) * inverse * (1.0 + scale_ref[:, columns]) + shift_ref[:, columns]
            largest = jnp.maximum(largest, jnp.max(jnp.abs(modulated), axis=0, keepdims=True))
            quant[at, columns] = jnp.clip(modulated * scale_up, -LIMIT, LIMIT).astype(jnp.bfloat16)
        return largest

    largest = lax.fori_loop(0, rows // block, norm_rows, jnp.zeros((1, width), jnp.float32))
    peak_ref[...] = jnp.broadcast_to(jnp.max(largest, axis=1, keepdims=True), peak_ref.shape)

    each_side(7, opposite_step)
    def core_arrivals(far_z, _):
        for order in range(4):
            slot = seq_of(far_z, 0, 1 - core)
            remote(
                wf.at[:, slot], wf.at[:, slot], cs.at[far_z, order], cr.at[far_z, order], partner_core
            ).wait_recv()
        return 0

    lax.fori_loop(0, NZ, core_arrivals, 0)
    depth = wf.shape[1] * wf.shape[2]

    def multiply(which, _):
        weight = wf[which].reshape(depth, width)
        product = jnp.dot(quant[...], weight, preferred_element_type=jnp.float32) * scale_down
        for head_here in range(width // HD):
            qkv_ref[which, head_here] = product[:, head_here * HD : (head_here + 1) * HD].astype(
                jnp.bfloat16
            )
        return 0

    lax.fori_loop(0, 3, multiply, 0)

    for copy in leg_one + leg_two:
        copy.wait_send()
    for kind in (0, 1):
        for which in (0, 1):
            x_copy(kind, which, 1).wait_send()
            x_copy(kind, which, -1).wait_send()
            x_forward(kind, which).wait_send()

    def drain(far_z, _):
        for direction in (1, -1):
            y_copy(far_z, direction).wait_send()

            @pl.when(inside(z_lo + direction) & ((z_lo - far_z) * direction >= 0))
            def _():
                for which in range(3):
                    z_copy(far_z, which, direction).wait_send()

        y_forward(far_z, 1).wait_send()
        for order in range(4):
            core_copy(far_z, y, order).wait_send()
        return 0

    lax.fori_loop(0, NZ, drain, 0)


def project(block_input, mod_shift, mod_scale, history, w_qkv):
    rows, width = block_input.shape
    three, depth, _ = w_qkv.shape
    seqs = lax.axis_size("seq")
    heads = lax.axis_size("head")
    dma = pltpu.SemaphoreType.DMA
    any_space = pl.BlockSpec(memory_space=pl.ANY)
    vmem = pl.BlockSpec(memory_space=pltpu.VMEM)
    return pl.pallas_call(
        project_kernel,
        out_shape=(
            jax.ShapeDtypeStruct((three, width // HD, rows, HD), jnp.bfloat16),
            jax.ShapeDtypeStruct((8, 128), jnp.float32),
        ),
        in_specs=[any_space, any_space, vmem, vmem, vmem],
        out_specs=(vmem, vmem),
        scratch_shapes=[
            pltpu.VMEM((heads, rows, width), jnp.bfloat16),
            pltpu.VMEM((three, seqs, depth, width), jnp.bfloat16),
            pltpu.VMEM((2, rows // 2, width), jnp.bfloat16),
            pltpu.VMEM((rows, heads * width), jnp.bfloat16),
            dma((2,)), dma((4,)), dma((2,)), dma((2,)),
            dma((2, 2, 3)), dma((2, 2, 3)),
            dma((2, NZ, 3)), dma((NZ, 3)),
            dma((2, NZ)), dma((2, NZ)),
            dma((NZ,)), dma((NZ,)),
            dma((NZ, 4)), dma((NZ, 4)),
        ],
        compiler_params=pltpu.CompilerParams(collective_id=0, has_side_effects=True),
        name="gather_project",
    )(block_input, w_qkv, mod_shift.reshape(1, -1), mod_scale.reshape(1, -1), history.reshape(1, -1))


def row_device(z_lo, row, head):
    return (z_lo * GRID_H + row, head)


def attention_kernel(
    pattern_ref, hist_ref, qkv_hbm, peak_hbm, grad_ref,
    out_ref, gqkv_ref, new_hist_ref,
    win0, win1, win2, query, gk, gv, parts, rows_in, zout, zin, near, far, ids, slots, repeats,
    local_sem, zs, zr, rs, rr, ms, mr, bs, br, fs, fr,
):
    z_lo, y, core, x, z_hi = place()
    head = x * 2 + z_hi
    row = y * 2 + core
    wins = (win0, win1, win2)
    heads = len(wins)
    tiles = query.shape[1]
    up, down = row_device(z_lo, row - 1, head), row_device(z_lo, row + 1, head)
    before, after = row_device(z_lo - 1, row, head), row_device(z_lo + 1, row, head)
    has_up, has_down = row > 0, row < GRID_H - 1
    has_before, has_after = z_lo > 0, z_lo < NZ - 1
    peers_row = [row_device(z_lo, (row + k) % GRID_H, head) for k in range(1, GRID_H)]
    peers_z = [row_device((z_lo + k) % NZ, row, head) for k in range(1, NZ)]
    greet([(d, None) for d in peers_row + peers_z])
    z_sides = ((0, has_before), (1, has_after))
    row_sides = ((0, has_up), (1, has_down))
    from_rows = ((0, has_down), (1, has_up))
    frames = ((0, has_before), (2, has_after), (1, None))

    def both(p, q):
        return p if q is None else p & q

    def slab(h, slot):
        return wins[h].at[:, pl.ds(slot * tiles, tiles)]

    def z_copy(h, side):
        target, frame = (before, 2) if side == 0 else (after, 0)
        return remote(
            qkv_hbm.at[pl.ds(1, 2), h], slab(h, frame * 3 + 1), zs.at[h, side], zr.at[h, side], target
        )

    def row_copy(h, frame, side):
        target = up if side == 0 else down
        source = qkv_hbm.at[pl.ds(1, 2), h] if frame == 1 else slab(h, frame * 3 + 1)
        return remote(
            source, slab(h, frame * 3 + (2 if side == 0 else 0)),
            rs.at[h, frame, side], rr.at[h, frame, side], target,
        )

    def own_slab(h):
        return pltpu.make_async_copy(qkv_hbm.at[pl.ds(1, 2), h], slab(h, 4), local_sem.at[h])

    def rows_out(h, frame):
        for side, valid in row_sides:

            @pl.when(valid)
            def _():
                row_copy(h, frame, side).start()

    def z_arrive(h):
        for frame, side, valid in ((2, 0, has_after), (0, 1, has_before)):

            @pl.when(valid)
            def _():
                z_copy(h, side).wait_recv()
                rows_out(h, frame)

    def rows_arrive(h):
        for frame, valid_frame in frames:
            for side, valid in from_rows:

                @pl.when(both(valid, valid_frame))
                def _():
                    row_copy(h, frame, side).wait_recv()

        own_slab(h).wait()

    own_peak = pltpu.make_async_copy(peak_hbm, near.at[row], local_sem.at[heads])
    own_far = pltpu.make_async_copy(near, far.at[z_lo], local_sem.at[heads + 1])
    own_query = pltpu.make_async_copy(qkv_hbm.at[0], query, local_sem.at[heads + 2])

    def max_near(k):
        return remote(peak_hbm, near.at[row], ms.at[0, k - 1], mr.at[0, k - 1], peers_row[k - 1])

    def max_far(k):
        return remote(near, far.at[z_lo], ms.at[1, k - 1], mr.at[1, k - 1], peers_z[k - 1])

    def back_row(h, frame, side):
        target = up if side == 0 else down
        return remote(
            parts.at[h, 0 if side == 0 else 2, frame], rows_in.at[h, side, frame],
            bs.at[h, frame, side], br.at[h, frame, side], target,
        )

    def back_z(h, side):
        target = before if side == 0 else after
        return remote(zout.at[h, side], zin.at[h, side], fs.at[h, side], fr.at[h, side], target)

    def back_rows_out(h, frame, valid_frame):
        for side, valid in row_sides:

            @pl.when(both(valid, valid_frame))
            def _():
                back_row(h, frame, side).start()

    def back_rows_arrive(h, frame, valid_frame):
        for side, valid in from_rows:

            @pl.when(both(valid, valid_frame))
            def _():
                back_row(h, frame, side).wait_recv()

    own_peak.start()
    own_query.start()
    for h in range(heads):
        own_slab(h).start()
        for side, valid in z_sides:

            @pl.when(valid)
            def _():
                z_copy(h, side).start()

        rows_out(h, 1)
        if h == 0:
            for k in range(1, GRID_H):
                max_near(k).start()

    def clear(buffer, side):
        for h in range(heads):
            buffer[h, side] = jnp.zeros(buffer.shape[2:], buffer.dtype)

    for side, valid in from_rows:

        @pl.when(jnp.logical_not(valid))
        def _():
            clear(rows_in, side)

    for side, valid in ((0, has_after), (1, has_before)):

        @pl.when(jnp.logical_not(valid))
        def _():
            clear(zin, side)

    for tile in range(tiles):
        gk[tile, KB] = jnp.zeros(gk.shape[2:], gk.dtype)
        gv[tile, KB] = jnp.zeros(gv.shape[2:], gv.dtype)

    for tile in range(tiles):
        for slot in range(KB):
            ids[tile, slot] = 0

    first_slab = (z_lo - 1) * GRID_H + row - 1

    def table(window, _):
        place_slab = first_slab + (window // 9) * GRID_H + (window // 3) % 3
        wanted = place_slab * tiles + window % 3
        for tile in range(tiles):
            found = jnp.int32(KB)
            for slot in range(KB):
                same = pattern_ref[tile, slot] == wanted
                found = jnp.where(same, slot, found)
                ids[tile, slot] = jnp.where(same, window, ids[tile, slot])
            slots[tile, window] = found
        return 0

    def count(slot, _):
        for tile in range(tiles):
            same = [(pattern_ref[tile, slot] == pattern_ref[tile, k]).astype(jnp.int32) for k in range(KB)]
            repeats[tile, slot] = sum(same).astype(jnp.float32)
        return 0

    z_arrive(0)
    lax.fori_loop(0, SLOTS * tiles, table, 0)
    lax.fori_loop(0, KB, count, 0)
    z_arrive(1)
    own_peak.wait()
    for k in range(1, GRID_H):
        max_near(k).wait_recv()
    own_far.start()
    for k in range(1, NZ):
        max_far(k).start()
    own_query.wait()
    rows_arrive(0)
    z_arrive(2)

    def one_head(h):
        win = wins[h]
        columns = slice(h * HD, (h + 1) * HD)

        def one_tile(tile, _):
            listed = [ids[tile, slot] for slot in range(KB)]
            q = query[h, tile]
            g = grad_ref[tile, :, columns]
            keys = jnp.concatenate([win[0, i] for i in listed], axis=0)
            values = jnp.concatenate([win[1, i] for i in listed], axis=0)
            scores = lax.dot_general(
                q, keys, (((1,), (1,)), ((), ())), preferred_element_type=jnp.float32
            )
            top = jnp.max(scores, axis=1, keepdims=True)
            weights = jnp.exp2((scores - top) * EXP2_SCALE)
            prob = weights * (1.0 / jnp.sum(weights, axis=1, keepdims=True))
            low = prob.astype(jnp.bfloat16)
            out = jnp.dot(low, values, preferred_element_type=jnp.float32)
            out_ref[tile, :, columns] = out.astype(jnp.bfloat16)
            gprob = lax.dot_general(
                g, values, (((1,), (1,)), ((), ())), preferred_element_type=jnp.float32
            )
            delta = jnp.sum(g.astype(jnp.float32) * out, axis=1, keepdims=True)
            gscore = (prob * (gprob - delta)).astype(jnp.bfloat16)
            gq = jnp.dot(gscore, keys, preferred_element_type=jnp.float32) * INV_ROOT
            gqkv_ref[0, tile, :, columns] = gq.astype(jnp.bfloat16)
            key_terms = lax.dot_general(
                gscore, q, (((0,), (0,)), ((), ())), preferred_element_type=jnp.float32
            )
            value_terms = lax.dot_general(
                low, g, (((0,), (0,)), ((), ())), preferred_element_type=jnp.float32
            )
            for slot in range(KB):
                span = slice(slot * TILE, (slot + 1) * TILE)
                often = repeats[tile, slot]
                gk[tile, slot] = key_terms[span] * (often * INV_ROOT)
                gv[tile, slot] = value_terms[span] * often
            return 0

        lax.fori_loop(0, tiles, one_tile, 0)
        waiting = None
        for frame, valid_frame in frames:

            def gather(at, _):
                step, column = at // tiles, at % tiles
                window = frame * 9 + at
                found = [slots[tile, window] for tile in range(tiles)]
                key_sum = gk[0, found[0]] + gk[1, found[1]] + gk[2, found[2]]
                value_sum = gv[0, found[0]] + gv[1, found[1]] + gv[2, found[2]]
                parts[h, step, frame, 0, column] = key_sum.astype(jnp.bfloat16)
                parts[h, step, frame, 1, column] = value_sum.astype(jnp.bfloat16)
                return 0

            lax.fori_loop(0, 3 * tiles, gather, 0)
            if waiting is not None:
                back_rows_out(h, *waiting)
            waiting = (frame, valid_frame)
        back_rows_out(h, *waiting)

    def total(h, frame, part, tile):
        return (
            parts[h, 1, frame, part, tile].astype(jnp.float32)
            + rows_in[h, 0, frame, part, tile].astype(jnp.float32)
            + rows_in[h, 1, frame, part, tile].astype(jnp.float32)
        )

    def reduce_rows(h):
        for frame, side, valid_frame in ((0, 0, has_before), (2, 1, has_after)):

            @pl.when(valid_frame)
            def _():
                back_rows_arrive(h, frame, None)

                def add(at, _):
                    part, tile = at // tiles, at % tiles
                    zout[h, side, part, tile] = total(h, frame, part, tile).astype(jnp.bfloat16)
                    return 0

                lax.fori_loop(0, 2 * tiles, add, 0)
                back_z(h, side).start()

    def finish(h):
        back_rows_arrive(h, 1, None)
        for side, valid in ((0, has_after), (1, has_before)):

            @pl.when(valid)
            def _():
                back_z(h, side).wait_recv()

        columns = slice(h * HD, (h + 1) * HD)

        def add(at, _):
            part, tile = at // tiles, at % tiles
            result = (
                total(h, 1, part, tile)
                + zin[h, 0, part, tile].astype(jnp.float32)
                + zin[h, 1, part, tile].astype(jnp.float32)
            )
            gqkv_ref[1 + part, tile, :, columns] = result.astype(jnp.bfloat16)
            return 0

        lax.fori_loop(0, 2 * tiles, add, 0)

    one_head(0)
    own_far.wait()
    for k in range(1, NZ):
        max_far(k).wait_recv()
    new_hist_ref[0] = jnp.max(far[...])
    for k in range(1, new_hist_ref.shape[0]):
        new_hist_ref[k] = hist_ref[k - 1]
    rows_arrive(1)
    one_head(1)
    reduce_rows(0)
    rows_arrive(2)
    one_head(2)
    reduce_rows(1)
    finish(0)
    reduce_rows(2)
    finish(1)
    finish(2)

    for h in range(heads):
        for side, valid in z_sides:

            @pl.when(valid)
            def _():
                z_copy(h, side).wait_send()
                back_z(h, side).wait_send()

        for frame, valid_frame in frames:
            inward = {0: has_before, 2: has_after, 1: None}[frame]
            for side, valid in row_sides:

                @pl.when(both(valid, inward))
                def _():
                    row_copy(h, frame, side).wait_send()
                    back_row(h, frame, side).wait_send()

    for k in range(1, GRID_H):
        max_near(k).wait_send()
    for k in range(1, NZ):
        max_far(k).wait_send()


def attention(pattern, history, qkv, peak, out_cotangent):
    _, heads, rows, _ = qkv.shape
    tiles = rows // TILE
    width = heads * HD
    dma = pltpu.SemaphoreType.DMA
    any_space = pl.BlockSpec(memory_space=pl.ANY)
    vmem = pl.BlockSpec(memory_space=pltpu.VMEM)
    smem = pl.BlockSpec(memory_space=pltpu.SMEM)
    tile = (TILE, HD)
    slab = (2, tiles) + tile
    return pl.pallas_call(
        attention_kernel,
        out_shape=(
            jax.ShapeDtypeStruct((tiles, TILE, width), jnp.bfloat16),
            jax.ShapeDtypeStruct((3, tiles, TILE, width), jnp.bfloat16),
            jax.ShapeDtypeStruct(history.shape, jnp.float32),
        ),
        in_specs=[smem, smem, any_space, any_space, vmem],
        out_specs=(vmem, vmem, smem),
        scratch_shapes=[pltpu.VMEM((2, SLOTS * tiles) + tile, jnp.bfloat16)] * heads
        + [
            pltpu.VMEM((heads, tiles) + tile, jnp.bfloat16),
            pltpu.VMEM((tiles, KB + 1) + tile, jnp.float32),
            pltpu.VMEM((tiles, KB + 1) + tile, jnp.float32),
            pltpu.VMEM((heads, 3, 3) + slab, jnp.bfloat16),
            pltpu.VMEM((heads, 2, 3) + slab, jnp.bfloat16),
            pltpu.VMEM((heads, 2) + slab, jnp.bfloat16),
            pltpu.VMEM((heads, 2) + slab, jnp.bfloat16),
            pltpu.VMEM((GRID_H, 8, 128), jnp.float32),
            pltpu.VMEM((NZ, GRID_H, 8, 128), jnp.float32),
            pltpu.SMEM((tiles, KB), jnp.int32),
            pltpu.SMEM((tiles, SLOTS * tiles), jnp.int32),
            pltpu.SMEM((tiles, KB), jnp.float32),
            dma((heads + 3,)),
            dma((heads, 2)), dma((heads, 2)),
            dma((heads, 3, 2)), dma((heads, 3, 2)),
            dma((2, 7)), dma((2, 7)),
            dma((heads, 3, 2)), dma((heads, 3, 2)),
            dma((heads, 2)), dma((heads, 2)),
        ],
        compiler_params=pltpu.CompilerParams(collective_id=1, has_side_effects=True),
        name="attention",
    )(
        pattern,
        history,
        qkv.reshape(3, heads, tiles, TILE, HD),
        peak,
        out_cotangent.reshape(tiles, TILE, width),
    )


def local(block_input, mod_shift, mod_scale, history, w_qkv, pattern, out_cotangent):
    rows, width = block_input.shape
    qkv, peak = project(block_input, mod_shift, mod_scale, history, w_qkv)
    attn_out, grad_qkv, new_history = attention(pattern, history, qkv, peak, out_cotangent)
    return (attn_out.reshape(rows, width), grad_qkv.reshape(3, rows, width), new_history)


def solution(mesh):
    placed = (
        P("seq", "head"),
        P(),
        P(),
        P(),
        P(None, "seq", "head"),
        P("seq", None),
        P("seq", "head"),
    )
    return jax.shard_map(
        local,
        mesh=mesh,
        in_specs=placed,
        out_specs=(P("seq", "head"), P(None, "seq", "head"), P()),
        check_vma=False,
    )
```

```python
import functools
import math

import jax
import jax.numpy as jnp
from jax import lax
from jax.experimental import pallas as pl
from jax.experimental.pallas import tpu as pltpu
from jax.sharding import PartitionSpec as P

HD = 128
TILE = 96
GRID_H = 8
NY = 4
NZ = 8
NX = 4
SLOTS = 9
KB = 12
LIMIT = 448.0
EPSILON = 1e-06
INV_ROOT = HD ** (-0.5)
EXP2_SCALE = INV_ROOT * math.log2(math.e)
MESH = pl.DeviceIdType.MESH
PIECES = 6
ORDER = (
    "s0", "s1", "s2", "x", "i0", "k", "i1", "z01", "z11", "i2", "z21", "z02", "a", "i3", "y00", "z12", "y10",
    "z22", "y20", "i4", "z03", "y01", "z13", "y11", "i5", "z23", "y21", "f0", "z04", "y02", "o00", "z14", "y12",
    "o10", "z24", "y22", "f1", "o20", "z05", "y03", "o01", "z15", "y13", "f2", "o11", "z25", "y23", "o21", "n0",
    "z06", "f3", "y04", "o02", "z16", "y14", "o12", "z26", "y24", "n1", "f4", "o22", "z07", "y05", "o03", "z17",
    "y15", "n2", "f5", "o13", "z27", "y25", "o23", "n3", "y06", "o04", "y16", "o14", "y26", "o24", "n4", "y07",
    "o05", "y17", "n5", "o15", "A", "y27", "o25", "o06", "o16", "o26", "o07", "o17", "o27", "c0", "p0", "h0",
    "c1", "p1", "h1", "c2", "p2", "h2", "Z0", "B", "Z1", "R0", "Z2", "C", "t00", "t01", "t02", "g0", "R1", "t10",
    "t11", "t12", "g1", "r0", "R2", "t20", "t21", "t22", "g2", "r1", "F0", "r2", "F1", "D", "F2",
)


def seq_of(z_lo, y, core):
    return (z_lo * NY + y) * 2 + core


def place():
    seq = lax.axis_index("seq")
    head = lax.axis_index("head")
    return seq // (2 * NY), (seq // 2) % NY, seq % 2, head // 2, head % 2


def remote(src, dst, send, recv, device):
    return pltpu.make_async_remote_copy(
        src_ref=src,
        dst_ref=dst,
        send_sem=send,
        recv_sem=recv,
        device_id=device,
        device_id_type=MESH,
    )


def greet(devices):
    barrier = pltpu.get_barrier_semaphore()
    for device, valid in devices:
        if valid is None:
            pl.semaphore_signal(barrier, inc=1, device_id=device, device_id_type=MESH)
        else:

            @pl.when(valid)
            def _():
                pl.semaphore_signal(barrier, inc=1, device_id=device, device_id_type=MESH)

    count = jnp.int32(sum(valid is None for _, valid in devices))
    for _, valid in devices:
        if valid is not None:
            count = count + valid.astype(jnp.int32)
    pl.semaphore_wait(barrier, count)


def row_device(z_lo, row, head):
    return (z_lo * GRID_H + row, head)


def block_kernel(
    pattern_ref, hist_smem, x_hbm, w_hbm, shift_ref, scale_ref, hist_ref, grad_ref,
    out_ref, gqkv_ref, new_hist_ref,
    xf, wf, quant, top, peak_own, qkv,
    win0, win1, win2, gk, gv, parts, rows_in, zout, zin, near, far, ids, slots, repeats,
    own_s, far_s, far_r, xs, xr, ps, pr, wzs, wzr, ys, yr, yos, yor, cs, cr,
    zs, zr, rs, rr, ms, mr, bs, br, fs, fr,
):
    heads = qkv.shape[0]
    z_lo, y, core, x, z_hi = place()
    seq = seq_of(z_lo, y, core)
    head = x * 2 + z_hi
    rows = xf.shape[1]
    piece = rows // PIECES

    def line_z(step):
        return (seq_of(z_lo + step, y, core), head)

    def ring_y(step):
        return (seq_of(z_lo, (y + step + NY) % NY, core), head)

    def ring_x(step):
        return (seq, ((x + step + NX) % NX) * 2 + z_hi)

    partner_core = (seq_of(z_lo, y, 1 - core), head)
    far_half = (seq, x * 2 + 1 - z_hi)
    peers_row = [row_device(z_lo, (y * 2 + core + k) % GRID_H, head) for k in range(1, GRID_H)]
    peers_z = [row_device((z_lo + k) % NZ, y * 2 + core, head) for k in range(1, NZ)]
    greet(
        [(d, None) for d in peers_row + peers_z]
        + [(far_half, None), (ring_x(1), None), (ring_x(-1), None), (ring_x(2), None)]
    )
    own_x = pltpu.make_async_copy(x_hbm, xf.at[head], own_s.at[heads])
    own_x.start()
    own_w = []
    for h in range(heads):
        copy = pltpu.make_async_copy(w_hbm.at[:, :, pl.ds(h * HD, HD)], wf.at[h, seq], own_s.at[h])
        copy.start()
        own_w.append(copy)

    def rows_of(ref, which):
        return ref.at[pl.ds(which * piece, piece)]

    def far_copy(which):
        return remote(
            rows_of(x_hbm, which), rows_of(xf.at[head], which), far_s.at[which], far_r.at[which], far_half
        )

    def far_arrival(which):
        ref = rows_of(xf.at[x * 2 + 1 - z_hi], which)
        return remote(ref, ref, far_s.at[which], far_r.at[which], far_half)

    def w_z(h, far_z, direction):
        ref = wf.at[h, seq_of(far_z, y, core)]
        side = 0 if direction > 0 else 1
        return remote(ref, ref, wzs.at[side, far_z, h], wzr.at[far_z, h], line_z(direction))

    def w_y(h, far_z, direction, arriving):
        source = (y - direction + NY) % NY if arriving else y
        ref = wf.at[h, seq_of(far_z, source, core)]
        side = 0 if direction > 0 else 1
        return remote(ref, ref, ys.at[side, far_z, h], yr.at[side, far_z, h], ring_y(direction))

    def w_opposite(h, far_z, direction):
        ref = wf.at[h, seq_of(far_z, (y - direction + NY) % NY, core)]
        return remote(ref, ref, yos.at[far_z, h], yor.at[far_z, h], ring_y(direction))

    def w_core(h, far_z, far_y, order):
        ref = wf.at[h, seq_of(far_z, far_y, core)]
        return remote(ref, ref, cs.at[far_z, order, h], cr.at[far_z, order, h], partner_core)

    def inside(far_z):
        return (far_z >= 0) & (far_z < NZ)

    def have_shard(h, far_z):
        w_y(h, far_z, 1, False).start()
        w_y(h, far_z, -1, False).start()
        w_core(h, far_z, y, 0).start()

    def each_side(step, act):
        if step == 0:
            act(z_lo)
            return
        for direction in (1, -1):
            far_z = z_lo - direction * step

            @pl.when(inside(far_z))
            def _():
                act(far_z)

    def own_shard(h):
        own_w[h].wait()
        for direction in (1, -1):

            @pl.when(inside(z_lo + direction))
            def _():
                w_z(h, z_lo, direction).start()

        have_shard(h, z_lo)

    def z_step(h, step):
        for direction in (1, -1):
            far_z = z_lo - direction * step

            @pl.when(inside(far_z))
            def _():
                w_z(h, far_z, direction).wait_recv()

                @pl.when(inside(z_lo + direction))
                def _():
                    w_z(h, far_z, direction).start()

                have_shard(h, far_z)

    def y_step(h, step):
        def act(far_z):
            for direction in (1, -1):
                w_y(h, far_z, direction, True).wait_recv()

                @pl.when(far_z % 2 == (0 if direction > 0 else 1))
                def _():
                    w_opposite(h, far_z, direction).start()

                w_core(h, far_z, (y - direction + NY) % NY, 1 if direction > 0 else 2).start()

        each_side(step, act)

    def opposite_step(h, step):
        def act(far_z):
            ref = wf.at[h, seq_of(far_z, (y + 2) % NY, core)]
            remote(ref, ref, yos.at[far_z, h], yor.at[far_z, h], ring_y(1)).wait_recv()
            w_core(h, far_z, (y + 2) % NY, 3).start()

        each_side(step, act)

    def core_step(h):
        def act(far_z, _):
            for order in range(4):
                ref = wf.at[h, seq_of(far_z, 0, 1 - core)]
                remote(
                    ref, ref, cs.at[far_z, order, h], cr.at[far_z, order, h], partner_core
                ).wait_recv()
            return 0

        lax.fori_loop(0, NZ, act, 0)

    steps_x = (1, -1, 2)

    def x_near(order, arriving):
        source = x - steps_x[order] if arriving else x
        ref = xf.at[((source + NX) % NX) * 2 + z_hi]
        return remote(ref, ref, xs.at[order], xr.at[order], ring_x(steps_x[order]))

    def x_far(which, order, arriving):
        source = x - steps_x[order] if arriving else x
        ref = rows_of(xf.at[((source + NX) % NX) * 2 + 1 - z_hi], which)
        return remote(ref, ref, ps.at[which, order], pr.at[which, order], ring_x(steps_x[order]))

    def far_step(which):
        far_arrival(which).wait_recv()
        for order in range(3):
            x_far(which, order, False).start()

    peak = jnp.max(hist_ref[...], axis=1, keepdims=True)
    scale_up = LIMIT / peak
    scale_down = peak / LIMIT
    chunks = xf.shape[0]
    width = xf.shape[2]
    features = chunks * width
    block = 16

    def norm_rows(index, largest):
        at = pl.ds(pl.multiple_of(index * block, block), block)
        total = jnp.zeros((block, width), jnp.float32)
        square = jnp.zeros((block, width), jnp.float32)
        for chunk in range(chunks):
            value = xf[chunk, at, :].astype(jnp.float32)
            total = total + value
            square = square + value * value
        mean = jnp.sum(total, axis=1, keepdims=True) * (1.0 / features)
        mean_square = jnp.sum(square, axis=1, keepdims=True) * (1.0 / features)
        inverse = lax.rsqrt(mean_square - mean * mean + EPSILON)
        for chunk in range(chunks):
            value = xf[chunk, at, :].astype(jnp.float32)
            columns = pl.ds(chunk * width, width)
            modulated = (value - mean) * inverse * (1.0 + scale_ref[:, columns]) + shift_ref[:, columns]
            largest = jnp.maximum(largest, jnp.max(jnp.abs(modulated), axis=0, keepdims=True))
            quant[at, columns] = jnp.clip(modulated * scale_up, -LIMIT, LIMIT).astype(jnp.bfloat16)
        return largest

    def norm_step(which):
        for order in range(3):
            x_far(which, order, True).wait_recv()
        per = piece // block
        top[...] = lax.fori_loop(which * per, (which + 1) * per, norm_rows, top[...])

    def near_step():
        for order in range(3):
            x_near(order, True).wait_recv()

    def near_out():
        own_x.wait()
        for order in range(3):
            x_near(order, False).start()

    def project(h):
        depth = wf.shape[1] * wf.shape[3]
        for which in range(3):
            weight = wf[h, :, which].reshape(depth, HD)
            product = jnp.dot(quant[...], weight, preferred_element_type=jnp.float32) * scale_down
            qkv[h, which] = product.astype(jnp.bfloat16).reshape(qkv.shape[2:])

    row = y * 2 + core
    wins = (win0, win1, win2)
    tiles = qkv.shape[2]
    up, down = row_device(z_lo, row - 1, head), row_device(z_lo, row + 1, head)
    before, after = row_device(z_lo - 1, row, head), row_device(z_lo + 1, row, head)
    has_up, has_down = row > 0, row < GRID_H - 1
    has_before, has_after = z_lo > 0, z_lo < NZ - 1
    z_sides = ((0, has_before), (1, has_after))
    row_sides = ((0, has_up), (1, has_down))
    from_rows = ((0, has_down), (1, has_up))
    frames = ((0, has_before), (2, has_after), (1, None))

    def both(p, q):
        return p if q is None else p & q

    def slab(h, slot):
        return wins[h].at[:, pl.ds(slot * tiles, tiles)]

    def z_copy(h, side):
        target, frame = (before, 2) if side == 0 else (after, 0)
        return remote(
            qkv.at[h, pl.ds(1, 2)], slab(h, frame * 3 + 1), zs.at[h, side], zr.at[h, side], target
        )

    def row_copy(h, frame, side):
        target = up if side == 0 else down
        source = qkv.at[h, pl.ds(1, 2)] if frame == 1 else slab(h, frame * 3 + 1)
        return remote(
            source, slab(h, frame * 3 + (2 if side == 0 else 0)),
            rs.at[h, frame, side], rr.at[h, frame, side], target,
        )

    def own_slab(h):
        return pltpu.make_async_copy(qkv.at[h, pl.ds(1, 2)], slab(h, 4), own_s.at[heads + 1 + h])

    def rows_out(h, frame):
        for side, valid in row_sides:

            @pl.when(valid)
            def _():
                row_copy(h, frame, side).start()

    def z_arrive(h):
        for frame, side, valid in ((2, 0, has_after), (0, 1, has_before)):

            @pl.when(valid)
            def _():
                z_copy(h, side).wait_recv()
                rows_out(h, frame)

    def rows_arrive(h):
        for frame, valid_frame in frames:
            for side, valid in from_rows:

                @pl.when(both(valid, valid_frame))
                def _():
                    row_copy(h, frame, side).wait_recv()

        own_slab(h).wait()

    own_peak = pltpu.make_async_copy(peak_own, near.at[row], own_s.at[2 * heads + 1])
    own_far = pltpu.make_async_copy(near, far.at[z_lo], own_s.at[2 * heads + 2])
    def max_near(k):
        return remote(peak_own, near.at[row], ms.at[0, k - 1], mr.at[0, k - 1], peers_row[k - 1])

    def max_far(k):
        return remote(near, far.at[z_lo], ms.at[1, k - 1], mr.at[1, k - 1], peers_z[k - 1])

    def back_row(h, frame, side):
        target = up if side == 0 else down
        return remote(
            parts.at[h, 0 if side == 0 else 2, frame], rows_in.at[h, side, frame],
            bs.at[h, frame, side], br.at[h, frame, side], target,
        )

    def back_z(h, side):
        target = before if side == 0 else after
        return remote(zout.at[h, side], zin.at[h, side], fs.at[h, side], fr.at[h, side], target)

    def back_rows_out(h, frame, valid_frame):
        for side, valid in row_sides:

            @pl.when(both(valid, valid_frame))
            def _():
                back_row(h, frame, side).start()

    def back_rows_arrive(h, frame, valid_frame):
        for side, valid in from_rows:

            @pl.when(both(valid, valid_frame))
            def _():
                back_row(h, frame, side).wait_recv()

    def halo_out(h):
        own_slab(h).start()
        for side, valid in z_sides:

            @pl.when(valid)
            def _():
                z_copy(h, side).start()

        rows_out(h, 1)

    def max_one():
        peak_own[...] = jnp.broadcast_to(jnp.max(top[...], axis=1, keepdims=True), peak_own.shape)

    def max_two():
        own_peak.start()
        for k in range(1, GRID_H):
            max_near(k).start()

    def max_three():
        own_peak.wait()
        for k in range(1, GRID_H):
            max_near(k).wait_recv()
        own_far.start()
        for k in range(1, NZ):
            max_far(k).start()

    def max_four():
        own_far.wait()
        for k in range(1, NZ):
            max_far(k).wait_recv()
        new_hist_ref[0] = jnp.max(far[...])
        for k in range(1, new_hist_ref.shape[0]):
            new_hist_ref[k] = hist_smem[k - 1]

    def prepare():
        def clear(buffer, side):
            for h in range(heads):
                buffer[h, side] = jnp.zeros(buffer.shape[2:], buffer.dtype)

        for side, valid in from_rows:

            @pl.when(jnp.logical_not(valid))
            def _():
                clear(rows_in, side)

        for side, valid in ((0, has_after), (1, has_before)):

            @pl.when(jnp.logical_not(valid))
            def _():
                clear(zin, side)

        for tile in range(tiles):
            gk[tile, KB] = jnp.zeros(gk.shape[2:], gk.dtype)
            gv[tile, KB] = jnp.zeros(gv.shape[2:], gv.dtype)

        for tile in range(tiles):
            for slot in range(KB):
                ids[tile, slot] = 0

        first_slab = (z_lo - 1) * GRID_H + row - 1

        def table(window, _):
            place_slab = first_slab + (window // 9) * GRID_H + (window // 3) % 3
            wanted = place_slab * tiles + window % 3
            for tile in range(tiles):
                found = jnp.int32(KB)
                for slot in range(KB):
                    same = pattern_ref[tile, slot] == wanted
                    found = jnp.where(same, slot, found)
                    ids[tile, slot] = jnp.where(same, window, ids[tile, slot])
                slots[tile, window] = found
            return 0

        def count(slot, _):
            for tile in range(tiles):
                same = [(pattern_ref[tile, slot] == pattern_ref[tile, k]).astype(jnp.int32) for k in range(KB)]
                repeats[tile, slot] = sum(same).astype(jnp.float32)
            return 0

        lax.fori_loop(0, SLOTS * tiles, table, 0)
        lax.fori_loop(0, KB, count, 0)

    def attend(h, tile):
        win = wins[h]
        columns = slice(h * HD, (h + 1) * HD)
        listed = [ids[tile, slot] for slot in range(KB)]
        q = qkv[h, 0, tile]
        g = grad_ref[tile, :, columns]
        keys = jnp.concatenate([win[0, i] for i in listed], axis=0)
        values = jnp.concatenate([win[1, i] for i in listed], axis=0)
        scores = lax.dot_general(
            q, keys, (((1,), (1,)), ((), ())), preferred_element_type=jnp.float32
        )
        top = jnp.max(scores, axis=1, keepdims=True)
        weights = jnp.exp2((scores - top) * EXP2_SCALE)
        prob = weights * (1.0 / jnp.sum(weights, axis=1, keepdims=True))
        low = prob.astype(jnp.bfloat16)
        out = jnp.dot(low, values, preferred_element_type=jnp.float32)
        out_ref[tile, :, columns] = out.astype(jnp.bfloat16)
        gprob = lax.dot_general(
            g, values, (((1,), (1,)), ((), ())), preferred_element_type=jnp.float32
        )
        delta = jnp.sum(g.astype(jnp.float32) * out, axis=1, keepdims=True)
        gscore = (prob * (gprob - delta)).astype(jnp.bfloat16)
        gq = jnp.dot(gscore, keys, preferred_element_type=jnp.float32) * INV_ROOT
        gqkv_ref[0, tile, :, columns] = gq.astype(jnp.bfloat16)
        key_terms = lax.dot_general(
            gscore, q, (((0,), (0,)), ((), ())), preferred_element_type=jnp.float32
        )
        value_terms = lax.dot_general(
            low, g, (((0,), (0,)), ((), ())), preferred_element_type=jnp.float32
        )
        for slot in range(KB):
            span = slice(slot * TILE, (slot + 1) * TILE)
            often = repeats[tile, slot]
            gk[tile, slot] = key_terms[span] * (often * INV_ROOT)
            gv[tile, slot] = value_terms[span] * often
    def give_back(h):
        waiting = None
        for frame, valid_frame in frames:

            def gather(at, _):
                step, column = at // tiles, at % tiles
                window = frame * 9 + at
                found = [slots[tile, window] for tile in range(tiles)]
                key_sum = gk[0, found[0]] + gk[1, found[1]] + gk[2, found[2]]
                value_sum = gv[0, found[0]] + gv[1, found[1]] + gv[2, found[2]]
                parts[h, step, frame, 0, column] = key_sum.astype(jnp.bfloat16)
                parts[h, step, frame, 1, column] = value_sum.astype(jnp.bfloat16)
                return 0

            lax.fori_loop(0, 3 * tiles, gather, 0)
            if waiting is not None:
                back_rows_out(h, *waiting)
            waiting = (frame, valid_frame)
        back_rows_out(h, *waiting)

    def total(h, frame, part, tile):
        return (
            parts[h, 1, frame, part, tile].astype(jnp.float32)
            + rows_in[h, 0, frame, part, tile].astype(jnp.float32)
            + rows_in[h, 1, frame, part, tile].astype(jnp.float32)
        )

    def reduce_rows(h):
        for frame, side, valid_frame in ((0, 0, has_before), (2, 1, has_after)):

            @pl.when(valid_frame)
            def _():
                back_rows_arrive(h, frame, None)

                def add(at, _):
                    part, tile = at // tiles, at % tiles
                    zout[h, side, part, tile] = total(h, frame, part, tile).astype(jnp.bfloat16)
                    return 0

                lax.fori_loop(0, 2 * tiles, add, 0)
                back_z(h, side).start()

    def finish(h):
        back_rows_arrive(h, 1, None)
        for side, valid in ((0, has_after), (1, has_before)):

            @pl.when(valid)
            def _():
                back_z(h, side).wait_recv()

        columns = slice(h * HD, (h + 1) * HD)

        def add(at, _):
            part, tile = at // tiles, at % tiles
            result = (
                total(h, 1, part, tile)
                + zin[h, 0, part, tile].astype(jnp.float32)
                + zin[h, 1, part, tile].astype(jnp.float32)
            )
            gqkv_ref[1 + part, tile, :, columns] = result.astype(jnp.bfloat16)
            return 0

        lax.fori_loop(0, 2 * tiles, add, 0)

    acts = {
        "s": own_shard,
        "z": z_step,
        "y": y_step,
        "o": opposite_step,
        "c": core_step,
        "p": project,
        "x": near_out,
        "a": near_step,
        "i": lambda which: far_copy(which).start(),
        "f": far_step,
        "n": norm_step,
        "h": halo_out,
        "Z": z_arrive,
        "R": rows_arrive,
        "t": attend,
        "g": give_back,
        "r": reduce_rows,
        "F": finish,
        "k": prepare,
        "A": max_one,
        "B": max_two,
        "C": max_three,
        "D": max_four,
    }
    top[...] = jnp.zeros_like(top)
    for item in ORDER:
        acts[item[0]](*[int(digit) for digit in item[1:]])

    for order in range(3):
        x_near(order, False).wait_send()
    for which in range(PIECES):
        far_copy(which).wait_send()
        for order in range(3):
            x_far(which, order, False).wait_send()

    def drain(far_z, _):
        for h in range(heads):
            for direction in (1, -1):
                w_y(h, far_z, direction, False).wait_send()

                @pl.when(inside(z_lo + direction) & ((z_lo - far_z) * direction >= 0))
                def _():
                    w_z(h, far_z, direction).wait_send()

            w_opposite(h, far_z, 1).wait_send()
            for order in range(4):
                w_core(h, far_z, y, order).wait_send()
        return 0

    lax.fori_loop(0, NZ, drain, 0)
    for h in range(heads):
        for side, valid in z_sides:

            @pl.when(valid)
            def _():
                z_copy(h, side).wait_send()
                back_z(h, side).wait_send()

        for frame, valid_frame in frames:
            inward = {0: has_before, 2: has_after, 1: None}[frame]
            for side, valid in row_sides:

                @pl.when(both(valid, inward))
                def _():
                    row_copy(h, frame, side).wait_send()
                    back_row(h, frame, side).wait_send()

    for k in range(1, GRID_H):
        max_near(k).wait_send()
    for k in range(1, NZ):
        max_far(k).wait_send()


def local(block_input, mod_shift, mod_scale, history, w_qkv, pattern, out_cotangent):
    rows, width = block_input.shape
    three, depth, _ = w_qkv.shape
    seqs = lax.axis_size("seq")
    chunks = lax.axis_size("head")
    heads = width // HD
    tiles = rows // TILE
    dma = pltpu.SemaphoreType.DMA
    any_space = pl.BlockSpec(memory_space=pl.ANY)
    vmem = pl.BlockSpec(memory_space=pltpu.VMEM)
    smem = pl.BlockSpec(memory_space=pltpu.SMEM)
    tile = (TILE, HD)
    slab = (2, tiles) + tile
    attn_out, grad_qkv, new_history = pl.pallas_call(
        block_kernel,
        out_shape=(
            jax.ShapeDtypeStruct((tiles, TILE, width), jnp.bfloat16),
            jax.ShapeDtypeStruct((3, tiles, TILE, width), jnp.bfloat16),
            jax.ShapeDtypeStruct(history.shape, jnp.float32),
        ),
        in_specs=[smem, smem, any_space, any_space, vmem, vmem, vmem, vmem],
        out_specs=(vmem, vmem, smem),
        scratch_shapes=[
            pltpu.VMEM((chunks, rows, width), jnp.bfloat16),
            pltpu.VMEM((heads, seqs, three, depth, HD), jnp.bfloat16),
            pltpu.VMEM((rows, chunks * width), jnp.bfloat16),
            pltpu.VMEM((1, width), jnp.float32),
            pltpu.VMEM((8, 128), jnp.float32),
            pltpu.VMEM((heads, 3, tiles) + tile, jnp.bfloat16),
        ]
        + [pltpu.VMEM((2, SLOTS * tiles) + tile, jnp.bfloat16)] * heads
        + [
            pltpu.VMEM((tiles, KB + 1) + tile, jnp.float32),
            pltpu.VMEM((tiles, KB + 1) + tile, jnp.float32),
            pltpu.VMEM((heads, 3, 3) + slab, jnp.bfloat16),
            pltpu.VMEM((heads, 2, 3) + slab, jnp.bfloat16),
            pltpu.VMEM((heads, 2) + slab, jnp.bfloat16),
            pltpu.VMEM((heads, 2) + slab, jnp.bfloat16),
            pltpu.VMEM((GRID_H, 8, 128), jnp.float32),
            pltpu.VMEM((NZ, GRID_H, 8, 128), jnp.float32),
            pltpu.SMEM((tiles, KB), jnp.int32),
            pltpu.SMEM((tiles, SLOTS * tiles), jnp.int32),
            pltpu.SMEM((tiles, KB), jnp.float32),
            dma((2 * heads + 3,)), dma((PIECES,)), dma((PIECES,)),
            dma((3,)), dma((3,)),
            dma((PIECES, 3)), dma((PIECES, 3)),
            dma((2, NZ, heads)), dma((NZ, heads)),
            dma((2, NZ, heads)), dma((2, NZ, heads)),
            dma((NZ, heads)), dma((NZ, heads)),
            dma((NZ, 4, heads)), dma((NZ, 4, heads)),
            dma((heads, 2)), dma((heads, 2)),
            dma((heads, 3, 2)), dma((heads, 3, 2)),
            dma((2, 7)), dma((2, 7)),
            dma((heads, 3, 2)), dma((heads, 3, 2)),
            dma((heads, 2)), dma((heads, 2)),
        ],
        compiler_params=pltpu.CompilerParams(collective_id=0, has_side_effects=True),
        name="block",
    )(
        pattern,
        history,
        block_input,
        w_qkv,
        mod_shift.reshape(1, -1),
        mod_scale.reshape(1, -1),
        history.reshape(1, -1),
        out_cotangent.reshape(tiles, TILE, width),
    )
    return (attn_out.reshape(rows, width), grad_qkv.reshape(3, rows, width), new_history)


def solution(mesh):
    placed = (
        P("seq", "head"),
        P(),
        P(),
        P(),
        P(None, "seq", "head"),
        P("seq", None),
        P("seq", "head"),
    )
    return jax.shard_map(
        local,
        mesh=mesh,
        in_specs=placed,
        out_specs=(P("seq", "head"), P(None, "seq", "head"), P()),
        check_vma=False,
    )
```

```python
import functools
import math

import jax
import jax.numpy as jnp
from jax import lax
from jax.experimental import pallas as pl
from jax.experimental.pallas import tpu as pltpu
from jax.sharding import PartitionSpec as P

HD = 128
TILE = 96
GRID_H = 8
NY = 4
NZ = 8
NX = 4
SLOTS = 9
KB = 12
LIMIT = 448.0
EPSILON = 1e-06
INV_ROOT = HD ** (-0.5)
EXP2_SCALE = INV_ROOT * math.log2(math.e)
MESH = pl.DeviceIdType.MESH
PIECES = 6
ORDER = (
    "s0", "s1", "s2", "x", "i0", "k", "i1", "z01", "z11", "i2", "z21", "z02", "a", "i3", "y00", "z12", "y10",
    "z22", "y20", "i4", "z03", "y01", "z13", "y11", "i5", "z23", "y21", "f0", "z04", "y02", "o00", "z14", "y12",
    "o10", "z24", "y22", "f1", "o20", "z05", "y03", "o01", "z15", "y13", "f2", "o11", "z25", "y23", "o21", "n0",
    "z06", "f3", "y04", "o02", "z16", "y14", "o12", "z26", "y24", "n1", "f4", "o22", "z07", "y05", "o03", "z17",
    "y15", "n2", "f5", "o13", "z27", "y25", "o23", "n3", "y06", "o04", "y16", "o14", "y26", "o24", "n4", "y07",
    "o05", "y17", "n5", "o15", "A", "y27", "o25", "o06", "o16", "o26", "o07", "o17", "o27", "c0", "p0", "h0",
    "c1", "p1", "h1", "c2", "p2", "h2", "Z0", "B", "Z1", "R0", "Z2", "C", "t00", "t01", "t02", "g0", "R1", "t10",
    "t11", "t12", "g1", "r0", "R2", "t20", "t21", "r1", "t22", "g2", "F0", "r2", "F1", "D", "F2",
)


def seq_of(z_lo, y, core):
    return (z_lo * NY + y) * 2 + core


def place():
    seq = lax.axis_index("seq")
    head = lax.axis_index("head")
    return seq // (2 * NY), (seq // 2) % NY, seq % 2, head // 2, head % 2


def remote(src, dst, send, recv, device):
    return pltpu.make_async_remote_copy(
        src_ref=src,
        dst_ref=dst,
        send_sem=send,
        recv_sem=recv,
        device_id=device,
        device_id_type=MESH,
    )


def greet(devices):
    barrier = pltpu.get_barrier_semaphore()
    for device, valid in devices:
        if valid is None:
            pl.semaphore_signal(barrier, inc=1, device_id=device, device_id_type=MESH)
        else:

            @pl.when(valid)
            def _():
                pl.semaphore_signal(barrier, inc=1, device_id=device, device_id_type=MESH)

    count = jnp.int32(sum(valid is None for _, valid in devices))
    for _, valid in devices:
        if valid is not None:
            count = count + valid.astype(jnp.int32)
    pl.semaphore_wait(barrier, count)


def row_device(z_lo, row, head):
    return (z_lo * GRID_H + row, head)


def block_kernel(
    pattern_ref, hist_smem, x_hbm, w_hbm, shift_ref, scale_ref, hist_ref, grad_ref,
    out_ref, gqkv_ref, new_hist_ref,
    xf, wf, quant, top, peak_own, qkv,
    win0, win1, win2, gk, gv, parts, rows_in, zout, zin, near, far, ids, slots, repeats,
    own_s, far_s, far_r, xs, xr, ps, pr, wzs, wzr, ys, yr, yos, yor, cs, cr,
    zs, zr, rs, rr, ms, mr, bs, br, fs, fr,
):
    heads = qkv.shape[0]
    z_lo, y, core, x, z_hi = place()
    seq = seq_of(z_lo, y, core)
    head = x * 2 + z_hi
    rows = xf.shape[1]
    piece = rows // PIECES

    def line_z(step):
        return (seq_of(z_lo + step, y, core), head)

    def ring_y(step):
        return (seq_of(z_lo, (y + step + NY) % NY, core), head)

    def ring_x(step):
        return (seq, ((x + step + NX) % NX) * 2 + z_hi)

    partner_core = (seq_of(z_lo, y, 1 - core), head)
    far_half = (seq, x * 2 + 1 - z_hi)
    peers_row = [row_device(z_lo, (y * 2 + core + k) % GRID_H, head) for k in range(1, GRID_H)]
    peers_z = [row_device((z_lo + k) % NZ, y * 2 + core, head) for k in range(1, NZ)]
    greet(
        [(d, None) for d in peers_row + peers_z]
        + [(far_half, None), (ring_x(1), None), (ring_x(-1), None), (ring_x(2), None)]
    )
    own_x = pltpu.make_async_copy(x_hbm, xf.at[head], own_s.at[heads])
    own_x.start()
    own_w = []
    for h in range(heads):
        copy = pltpu.make_async_copy(w_hbm.at[:, :, pl.ds(h * HD, HD)], wf.at[h, seq], own_s.at[h])
        copy.start()
        own_w.append(copy)

    def rows_of(ref, which):
        return ref.at[pl.ds(which * piece, piece)]

    def far_copy(which):
        return remote(
            rows_of(x_hbm, which), rows_of(xf.at[head], which), far_s.at[which], far_r.at[which], far_half
        )

    def far_arrival(which):
        ref = rows_of(xf.at[x * 2 + 1 - z_hi], which)
        return remote(ref, ref, far_s.at[which], far_r.at[which], far_half)

    def w_z(h, far_z, direction):
        ref = wf.at[h, seq_of(far_z, y, core)]
        side = 0 if direction > 0 else 1
        return remote(ref, ref, wzs.at[side, far_z, h], wzr.at[far_z, h], line_z(direction))

    def w_y(h, far_z, direction, arriving):
        source = (y - direction + NY) % NY if arriving else y
        ref = wf.at[h, seq_of(far_z, source, core)]
        side = 0 if direction > 0 else 1
        return remote(ref, ref, ys.at[side, far_z, h], yr.at[side, far_z, h], ring_y(direction))

    def w_opposite(h, far_z, direction):
        ref = wf.at[h, seq_of(far_z, (y - direction + NY) % NY, core)]
        return remote(ref, ref, yos.at[far_z, h], yor.at[far_z, h], ring_y(direction))

    def w_core(h, far_z, far_y, order):
        ref = wf.at[h, seq_of(far_z, far_y, core)]
        return remote(ref, ref, cs.at[far_z, order, h], cr.at[far_z, order, h], partner_core)

    def inside(far_z):
        return (far_z >= 0) & (far_z < NZ)

    def have_shard(h, far_z):
        w_y(h, far_z, 1, False).start()
        w_y(h, far_z, -1, False).start()
        w_core(h, far_z, y, 0).start()

    def each_side(step, act):
        if step == 0:
            act(z_lo)
            return
        for direction in (1, -1):
            far_z = z_lo - direction * step

            @pl.when(inside(far_z))
            def _():
                act(far_z)

    def own_shard(h):
        own_w[h].wait()
        for direction in (1, -1):

            @pl.when(inside(z_lo + direction))
            def _():
                w_z(h, z_lo, direction).start()

        have_shard(h, z_lo)

    def z_step(h, step):
        for direction in (1, -1):
            far_z = z_lo - direction * step

            @pl.when(inside(far_z))
            def _():
                w_z(h, far_z, direction).wait_recv()

                @pl.when(inside(z_lo + direction))
                def _():
                    w_z(h, far_z, direction).start()

                have_shard(h, far_z)

    def y_step(h, step):
        def act(far_z):
            for direction in (1, -1):
                w_y(h, far_z, direction, True).wait_recv()

                @pl.when(far_z % 2 == (0 if direction > 0 else 1))
                def _():
                    w_opposite(h, far_z, direction).start()

                w_core(h, far_z, (y - direction + NY) % NY, 1 if direction > 0 else 2).start()

        each_side(step, act)

    def opposite_step(h, step):
        def act(far_z):
            ref = wf.at[h, seq_of(far_z, (y + 2) % NY, core)]
            remote(ref, ref, yos.at[far_z, h], yor.at[far_z, h], ring_y(1)).wait_recv()
            w_core(h, far_z, (y + 2) % NY, 3).start()

        each_side(step, act)

    def core_step(h):
        def act(far_z, _):
            for order in range(4):
                ref = wf.at[h, seq_of(far_z, 0, 1 - core)]
                remote(
                    ref, ref, cs.at[far_z, order, h], cr.at[far_z, order, h], partner_core
                ).wait_recv()
            return 0

        lax.fori_loop(0, NZ, act, 0)

    steps_x = (1, -1, 2)

    def x_near(order, arriving):
        source = x - steps_x[order] if arriving else x
        ref = xf.at[((source + NX) % NX) * 2 + z_hi]
        return remote(ref, ref, xs.at[order], xr.at[order], ring_x(steps_x[order]))

    def x_far(which, order, arriving):
        source = x - steps_x[order] if arriving else x
        ref = rows_of(xf.at[((source + NX) % NX) * 2 + 1 - z_hi], which)
        return remote(ref, ref, ps.at[which, order], pr.at[which, order], ring_x(steps_x[order]))

    def far_step(which):
        far_arrival(which).wait_recv()
        for order in range(3):
            x_far(which, order, False).start()

    peak = jnp.max(hist_ref[...], axis=1, keepdims=True)
    scale_up = LIMIT / peak
    scale_down = peak / LIMIT
    chunks = xf.shape[0]
    width = xf.shape[2]
    features = chunks * width
    block = 16

    def norm_rows(index, largest):
        at = pl.ds(pl.multiple_of(index * block, block), block)
        total = jnp.zeros((block, width), jnp.float32)
        square = jnp.zeros((block, width), jnp.float32)
        for chunk in range(chunks):
            value = xf[chunk, at, :].astype(jnp.float32)
            total = total + value
            square = square + value * value
        mean = jnp.sum(total, axis=1, keepdims=True) * (1.0 / features)
        mean_square = jnp.sum(square, axis=1, keepdims=True) * (1.0 / features)
        inverse = lax.rsqrt(mean_square - mean * mean + EPSILON)
        for chunk in range(chunks):
            value = xf[chunk, at, :].astype(jnp.float32)
            columns = pl.ds(chunk * width, width)
            modulated = (value - mean) * inverse * (1.0 + scale_ref[:, columns]) + shift_ref[:, columns]
            largest = jnp.maximum(largest, jnp.max(jnp.abs(modulated), axis=0, keepdims=True))
            quant[at, columns] = jnp.clip(modulated * scale_up, -LIMIT, LIMIT).astype(jnp.bfloat16)
        return largest

    def norm_step(which):
        for order in range(3):
            x_far(which, order, True).wait_recv()
        per = piece // block
        top[...] = lax.fori_loop(which * per, (which + 1) * per, norm_rows, top[...])

    def near_step():
        for order in range(3):
            x_near(order, True).wait_recv()

    def near_out():
        own_x.wait()
        for order in range(3):
            x_near(order, False).start()

    def project(h):
        depth = wf.shape[1] * wf.shape[3]
        for which in range(3):
            weight = wf[h, :, which].reshape(depth, HD)
            product = jnp.dot(quant[...], weight, preferred_element_type=jnp.float32) * scale_down
            qkv[h, which] = product.astype(jnp.bfloat16).reshape(qkv.shape[2:])

    row = y * 2 + core
    wins = (win0, win1, win2)
    tiles = qkv.shape[2]
    up, down = row_device(z_lo, row - 1, head), row_device(z_lo, row + 1, head)
    before, after = row_device(z_lo - 1, row, head), row_device(z_lo + 1, row, head)
    has_up, has_down = row > 0, row < GRID_H - 1
    has_before, has_after = z_lo > 0, z_lo < NZ - 1
    z_sides = ((0, has_before), (1, has_after))
    row_sides = ((0, has_up), (1, has_down))
    from_rows = ((0, has_down), (1, has_up))
    frames = ((0, has_before), (2, has_after), (1, None))

    def both(p, q):
        return p if q is None else p & q

    def slab(h, slot):
        return wins[h].at[:, pl.ds(slot * tiles, tiles)]

    def z_copy(h, side):
        target, frame = (before, 2) if side == 0 else (after, 0)
        return remote(
            qkv.at[h, pl.ds(1, 2)], slab(h, frame * 3 + 1), zs.at[h, side], zr.at[h, side], target
        )

    def row_copy(h, frame, side):
        target = up if side == 0 else down
        source = qkv.at[h, pl.ds(1, 2)] if frame == 1 else slab(h, frame * 3 + 1)
        return remote(
            source, slab(h, frame * 3 + (2 if side == 0 else 0)),
            rs.at[h, frame, side], rr.at[h, frame, side], target,
        )

    def own_slab(h):
        return pltpu.make_async_copy(qkv.at[h, pl.ds(1, 2)], slab(h, 4), own_s.at[heads + 1 + h])

    def rows_out(h, frame):
        for side, valid in row_sides:

            @pl.when(valid)
            def _():
                row_copy(h, frame, side).start()

    def z_arrive(h):
        for frame, side, valid in ((2, 0, has_after), (0, 1, has_before)):

            @pl.when(valid)
            def _():
                z_copy(h, side).wait_recv()
                rows_out(h, frame)

    def rows_arrive(h):
        for frame, valid_frame in frames:
            for side, valid in from_rows:

                @pl.when(both(valid, valid_frame))
                def _():
                    row_copy(h, frame, side).wait_recv()

        own_slab(h).wait()

    own_peak = pltpu.make_async_copy(peak_own, near.at[row], own_s.at[2 * heads + 1])
    own_far = pltpu.make_async_copy(near, far.at[z_lo], own_s.at[2 * heads + 2])
    def max_near(k):
        return remote(peak_own, near.at[row], ms.at[0, k - 1], mr.at[0, k - 1], peers_row[k - 1])

    def max_far(k):
        return remote(near, far.at[z_lo], ms.at[1, k - 1], mr.at[1, k - 1], peers_z[k - 1])

    def back_row(h, frame, side):
        target = up if side == 0 else down
        return remote(
            parts.at[h, 0 if side == 0 else 2, frame], rows_in.at[h, side, frame],
            bs.at[h, frame, side], br.at[h, frame, side], target,
        )

    def back_z(h, side):
        target = before if side == 0 else after
        return remote(zout.at[h, side], zin.at[h, side], fs.at[h, side], fr.at[h, side], target)

    def back_rows_out(h, frame, valid_frame):
        for side, valid in row_sides:

            @pl.when(both(valid, valid_frame))
            def _():
                back_row(h, frame, side).start()

    def back_rows_arrive(h, frame, valid_frame):
        for side, valid in from_rows:

            @pl.when(both(valid, valid_frame))
            def _():
                back_row(h, frame, side).wait_recv()

    def halo_out(h):
        own_slab(h).start()
        for side, valid in z_sides:

            @pl.when(valid)
            def _():
                z_copy(h, side).start()

        rows_out(h, 1)

    def max_one():
        peak_own[...] = jnp.broadcast_to(jnp.max(top[...], axis=1, keepdims=True), peak_own.shape)

    def max_two():
        own_peak.start()
        for k in range(1, GRID_H):
            max_near(k).start()

    def max_three():
        own_peak.wait()
        for k in range(1, GRID_H):
            max_near(k).wait_recv()
        own_far.start()
        for k in range(1, NZ):
            max_far(k).start()

    def max_four():
        own_far.wait()
        for k in range(1, NZ):
            max_far(k).wait_recv()
        new_hist_ref[0] = jnp.max(far[...])
        for k in range(1, new_hist_ref.shape[0]):
            new_hist_ref[k] = hist_smem[k - 1]

    def prepare():
        def clear(buffer, side):
            for h in range(heads):
                buffer[h, side] = jnp.zeros(buffer.shape[2:], buffer.dtype)

        for side, valid in from_rows:

            @pl.when(jnp.logical_not(valid))
            def _():
                clear(rows_in, side)

        for side, valid in ((0, has_after), (1, has_before)):

            @pl.when(jnp.logical_not(valid))
            def _():
                clear(zin, side)

        for tile in range(tiles):
            gk[tile, KB] = jnp.zeros(gk.shape[2:], gk.dtype)
            gv[tile, KB] = jnp.zeros(gv.shape[2:], gv.dtype)

        for tile in range(tiles):
            for slot in range(KB):
                ids[tile, slot] = 0

        first_slab = (z_lo - 1) * GRID_H + row - 1

        def table(window, _):
            place_slab = first_slab + (window // 9) * GRID_H + (window // 3) % 3
            wanted = place_slab * tiles + window % 3
            for tile in range(tiles):
                found = jnp.int32(KB)
                for slot in range(KB):
                    same = pattern_ref[tile, slot] == wanted
                    found = jnp.where(same, slot, found)
                    ids[tile, slot] = jnp.where(same, window, ids[tile, slot])
                slots[tile, window] = found
            return 0

        def count(slot, _):
            for tile in range(tiles):
                same = [(pattern_ref[tile, slot] == pattern_ref[tile, k]).astype(jnp.int32) for k in range(KB)]
                repeats[tile, slot] = sum(same).astype(jnp.float32)
            return 0

        lax.fori_loop(0, SLOTS * tiles, table, 0)
        lax.fori_loop(0, KB, count, 0)

    def attend(h, tile):
        win = wins[h]
        columns = slice(h * HD, (h + 1) * HD)
        listed = [ids[tile, slot] for slot in range(KB)]
        q = qkv[h, 0, tile]
        g = grad_ref[tile, :, columns]
        keys = jnp.concatenate([win[0, i] for i in listed], axis=0)
        values = jnp.concatenate([win[1, i] for i in listed], axis=0)
        scores = lax.dot_general(
            q, keys, (((1,), (1,)), ((), ())), preferred_element_type=jnp.float32
        )
        top = jnp.max(scores, axis=1, keepdims=True)
        weights = jnp.exp2((scores - top) * EXP2_SCALE)
        prob = weights * (1.0 / jnp.sum(weights, axis=1, keepdims=True))
        low = prob.astype(jnp.bfloat16)
        out = jnp.dot(low, values, preferred_element_type=jnp.float32)
        out_ref[tile, :, columns] = out.astype(jnp.bfloat16)
        gprob = lax.dot_general(
            g, values, (((1,), (1,)), ((), ())), preferred_element_type=jnp.float32
        )
        delta = jnp.sum(g.astype(jnp.float32) * out, axis=1, keepdims=True)
        gscore = (prob * (gprob - delta)).astype(jnp.bfloat16)
        gq = jnp.dot(gscore, keys, preferred_element_type=jnp.float32) * INV_ROOT
        gqkv_ref[0, tile, :, columns] = gq.astype(jnp.bfloat16)
        key_terms = lax.dot_general(
            gscore, q, (((0,), (0,)), ((), ())), preferred_element_type=jnp.float32
        )
        value_terms = lax.dot_general(
            low, g, (((0,), (0,)), ((), ())), preferred_element_type=jnp.float32
        )
        for slot in range(KB):
            span = slice(slot * TILE, (slot + 1) * TILE)
            often = repeats[tile, slot]
            gk[tile, slot] = key_terms[span] * (often * INV_ROOT)
            gv[tile, slot] = value_terms[span] * often
    def give_back(h):
        waiting = None
        for frame, valid_frame in frames:

            def gather(at, _):
                step, column = at // tiles, at % tiles
                window = frame * 9 + at
                found = [slots[tile, window] for tile in range(tiles)]
                key_sum = gk[0, found[0]] + gk[1, found[1]] + gk[2, found[2]]
                value_sum = gv[0, found[0]] + gv[1, found[1]] + gv[2, found[2]]
                parts[h, step, frame, 0, column] = key_sum.astype(jnp.bfloat16)
                parts[h, step, frame, 1, column] = value_sum.astype(jnp.bfloat16)
                return 0

            lax.fori_loop(0, 3 * tiles, gather, 0)
            if waiting is not None:
                back_rows_out(h, *waiting)
            waiting = (frame, valid_frame)
        back_rows_out(h, *waiting)

    def total(h, frame, part, tile):
        return (
            parts[h, 1, frame, part, tile].astype(jnp.float32)
            + rows_in[h, 0, frame, part, tile].astype(jnp.float32)
            + rows_in[h, 1, frame, part, tile].astype(jnp.float32)
        )

    def reduce_rows(h):
        for frame, side, valid_frame in ((0, 0, has_before), (2, 1, has_after)):

            @pl.when(valid_frame)
            def _():
                back_rows_arrive(h, frame, None)

                def add(at, _):
                    part, tile = at // tiles, at % tiles
                    zout[h, side, part, tile] = total(h, frame, part, tile).astype(jnp.bfloat16)
                    return 0

                lax.fori_loop(0, 2 * tiles, add, 0)
                back_z(h, side).start()

    def finish(h):
        back_rows_arrive(h, 1, None)
        for side, valid in ((0, has_after), (1, has_before)):

            @pl.when(valid)
            def _():
                back_z(h, side).wait_recv()

        columns = slice(h * HD, (h + 1) * HD)

        def add(at, _):
            part, tile = at // tiles, at % tiles
            result = (
                total(h, 1, part, tile)
                + zin[h, 0, part, tile].astype(jnp.float32)
                + zin[h, 1, part, tile].astype(jnp.float32)
            )
            gqkv_ref[1 + part, tile, :, columns] = result.astype(jnp.bfloat16)
            return 0

        lax.fori_loop(0, 2 * tiles, add, 0)

    acts = {
        "s": own_shard,
        "z": z_step,
        "y": y_step,
        "o": opposite_step,
        "c": core_step,
        "p": project,
        "x": near_out,
        "a": near_step,
        "i": lambda which: far_copy(which).start(),
        "f": far_step,
        "n": norm_step,
        "h": halo_out,
        "Z": z_arrive,
        "R": rows_arrive,
        "t": attend,
        "g": give_back,
        "r": reduce_rows,
        "F": finish,
        "k": prepare,
        "A": max_one,
        "B": max_two,
        "C": max_three,
        "D": max_four,
    }
    top[...] = jnp.zeros_like(top)
    for item in ORDER:
        acts[item[0]](*[int(digit) for digit in item[1:]])

    for order in range(3):
        x_near(order, False).wait_send()
    for which in range(PIECES):
        far_copy(which).wait_send()
        for order in range(3):
            x_far(which, order, False).wait_send()

    def drain(far_z, _):
        for h in range(heads):
            for direction in (1, -1):
                w_y(h, far_z, direction, False).wait_send()

                @pl.when(inside(z_lo + direction) & ((z_lo - far_z) * direction >= 0))
                def _():
                    w_z(h, far_z, direction).wait_send()

            w_opposite(h, far_z, 1).wait_send()
            for order in range(4):
                w_core(h, far_z, y, order).wait_send()
        return 0

    lax.fori_loop(0, NZ, drain, 0)
    for h in range(heads):
        for side, valid in z_sides:

            @pl.when(valid)
            def _():
                z_copy(h, side).wait_send()
                back_z(h, side).wait_send()

        for frame, valid_frame in frames:
            inward = {0: has_before, 2: has_after, 1: None}[frame]
            for side, valid in row_sides:

                @pl.when(both(valid, inward))
                def _():
                    row_copy(h, frame, side).wait_send()
                    back_row(h, frame, side).wait_send()

    for k in range(1, GRID_H):
        max_near(k).wait_send()
    for k in range(1, NZ):
        max_far(k).wait_send()


def local(block_input, mod_shift, mod_scale, history, w_qkv, pattern, out_cotangent):
    rows, width = block_input.shape
    three, depth, _ = w_qkv.shape
    seqs = lax.axis_size("seq")
    chunks = lax.axis_size("head")
    heads = width // HD
    tiles = rows // TILE
    dma = pltpu.SemaphoreType.DMA
    any_space = pl.BlockSpec(memory_space=pl.ANY)
    vmem = pl.BlockSpec(memory_space=pltpu.VMEM)
    smem = pl.BlockSpec(memory_space=pltpu.SMEM)
    tile = (TILE, HD)
    slab = (2, tiles) + tile
    attn_out, grad_qkv, new_history = pl.pallas_call(
        block_kernel,
        out_shape=(
            jax.ShapeDtypeStruct((tiles, TILE, width), jnp.bfloat16),
            jax.ShapeDtypeStruct((3, tiles, TILE, width), jnp.bfloat16),
            jax.ShapeDtypeStruct(history.shape, jnp.float32),
        ),
        in_specs=[smem, smem, any_space, any_space, vmem, vmem, vmem, vmem],
        out_specs=(vmem, vmem, smem),
        scratch_shapes=[
            pltpu.VMEM((chunks, rows, width), jnp.bfloat16),
            pltpu.VMEM((heads, seqs, three, depth, HD), jnp.bfloat16),
            pltpu.VMEM((rows, chunks * width), jnp.bfloat16),
            pltpu.VMEM((1, width), jnp.float32),
            pltpu.VMEM((8, 128), jnp.float32),
            pltpu.VMEM((heads, 3, tiles) + tile, jnp.bfloat16),
        ]
        + [pltpu.VMEM((2, SLOTS * tiles) + tile, jnp.bfloat16)] * heads
        + [
            pltpu.VMEM((tiles, KB + 1) + tile, jnp.float32),
            pltpu.VMEM((tiles, KB + 1) + tile, jnp.float32),
            pltpu.VMEM((heads, 3, 3) + slab, jnp.bfloat16),
            pltpu.VMEM((heads, 2, 3) + slab, jnp.bfloat16),
            pltpu.VMEM((heads, 2) + slab, jnp.bfloat16),
            pltpu.VMEM((heads, 2) + slab, jnp.bfloat16),
            pltpu.VMEM((GRID_H, 8, 128), jnp.float32),
            pltpu.VMEM((NZ, GRID_H, 8, 128), jnp.float32),
            pltpu.SMEM((tiles, KB), jnp.int32),
            pltpu.SMEM((tiles, SLOTS * tiles), jnp.int32),
            pltpu.SMEM((tiles, KB), jnp.float32),
            dma((2 * heads + 3,)), dma((PIECES,)), dma((PIECES,)),
            dma((3,)), dma((3,)),
            dma((PIECES, 3)), dma((PIECES, 3)),
            dma((2, NZ, heads)), dma((NZ, heads)),
            dma((2, NZ, heads)), dma((2, NZ, heads)),
            dma((NZ, heads)), dma((NZ, heads)),
            dma((NZ, 4, heads)), dma((NZ, 4, heads)),
            dma((heads, 2)), dma((heads, 2)),
            dma((heads, 3, 2)), dma((heads, 3, 2)),
            dma((2, 7)), dma((2, 7)),
            dma((heads, 3, 2)), dma((heads, 3, 2)),
            dma((heads, 2)), dma((heads, 2)),
        ],
        compiler_params=pltpu.CompilerParams(collective_id=0, has_side_effects=True),
        name="block",
    )(
        pattern,
        history,
        block_input,
        w_qkv,
        mod_shift.reshape(1, -1),
        mod_scale.reshape(1, -1),
        history.reshape(1, -1),
        out_cotangent.reshape(tiles, TILE, width),
    )
    return (attn_out.reshape(rows, width), grad_qkv.reshape(3, rows, width), new_history)


def solution(mesh):
    placed = (
        P("seq", "head"),
        P(),
        P(),
        P(),
        P(None, "seq", "head"),
        P("seq", None),
        P("seq", "head"),
    )
    return jax.shard_map(
        local,
        mesh=mesh,
        in_specs=placed,
        out_specs=(P("seq", "head"), P(None, "seq", "head"), P()),
        check_vma=False,
    )
```

```python
import functools
import math

import jax
import jax.numpy as jnp
from jax import lax
from jax.experimental import pallas as pl
from jax.experimental.pallas import tpu as pltpu
from jax.sharding import PartitionSpec as P

HD = 128
TILE = 96
GRID_H = 8
NY = 4
NZ = 8
NX = 4
SLOTS = 9
KB = 12
LIMIT = 448.0
EPSILON = 1e-06
INV_ROOT = HD ** (-0.5)
EXP2_SCALE = INV_ROOT * math.log2(math.e)
MESH = pl.DeviceIdType.MESH
PIECES = 6
ORDER = (
    "s0", "s1", "s2", "x", "i0", "k", "i1", "i2", "z01", "z11", "i3", "z21", "i4", "z02", "a", "y00", "z12",
    "y10", "i5", "z22", "y20", "z03", "y01", "z13", "y11", "z23", "y21", "f0", "z04", "y02", "o00", "z14", "y12",
    "f1", "o10", "z24", "y22", "o20", "f2", "z05", "y03", "o01", "z15", "y13", "f3", "o11", "z25", "y23", "o21",
    "n0", "f4", "z06", "y04", "o02", "z16", "y14", "n1", "f5", "o12", "z26", "y24", "o22", "n2", "z07", "y05",
    "o03", "z17", "y15", "n3", "o13", "z27", "y25", "o23", "n4", "y06", "o04", "y16", "n5", "o14", "A", "y26",
    "o24", "y07", "o05", "y17", "o15", "y27", "o25", "o06", "o16", "o26", "o07", "o17", "o27", "c0", "p0", "h0",
    "c1", "p1", "h1", "c2", "p2", "h2", "Z0", "B", "Z1", "R0", "Z2", "C", "t00", "t01", "t02", "g0", "R1", "t10",
    "t11", "t12", "g1", "r0", "R2", "t20", "t21", "t22", "g2", "r1", "F0", "r2", "F1", "D", "F2",
)


def seq_of(z_lo, y, core):
    return (z_lo * NY + y) * 2 + core


def place():
    seq = lax.axis_index("seq")
    head = lax.axis_index("head")
    return seq // (2 * NY), (seq // 2) % NY, seq % 2, head // 2, head % 2


def remote(src, dst, send, recv, device):
    return pltpu.make_async_remote_copy(
        src_ref=src,
        dst_ref=dst,
        send_sem=send,
        recv_sem=recv,
        device_id=device,
        device_id_type=MESH,
    )


def greet(devices):
    barrier = pltpu.get_barrier_semaphore()
    for device, valid in devices:
        if valid is None:
            pl.semaphore_signal(barrier, inc=1, device_id=device, device_id_type=MESH)
        else:

            @pl.when(valid)
            def _():
                pl.semaphore_signal(barrier, inc=1, device_id=device, device_id_type=MESH)

    count = jnp.int32(sum(valid is None for _, valid in devices))
    for _, valid in devices:
        if valid is not None:
            count = count + valid.astype(jnp.int32)
    pl.semaphore_wait(barrier, count)


def row_device(z_lo, row, head):
    return (z_lo * GRID_H + row, head)


def block_kernel(
    pattern_ref, hist_smem, x_hbm, w_hbm, shift_ref, scale_ref, hist_ref, grad_ref,
    out_ref, gqkv_ref, new_hist_ref,
    xf, wf, quant, top, peak_own, qkv,
    win0, win1, win2, gk, gv, parts, rows_in, zout, zin, near, far, ids, slots, repeats,
    own_s, far_s, far_r, xs, xr, ps, pr, wzs, wzr, ys, yr, yos, yor, cs, cr,
    zs, zr, rs, rr, ms, mr, bs, br, fs, fr,
):
    heads = qkv.shape[0]
    z_lo, y, core, x, z_hi = place()
    seq = seq_of(z_lo, y, core)
    head = x * 2 + z_hi
    rows = xf.shape[1]
    piece = rows // PIECES

    def line_z(step):
        return (seq_of(z_lo + step, y, core), head)

    def ring_y(step):
        return (seq_of(z_lo, (y + step + NY) % NY, core), head)

    def ring_x(step):
        return (seq, ((x + step + NX) % NX) * 2 + z_hi)

    partner_core = (seq_of(z_lo, y, 1 - core), head)
    far_half = (seq, x * 2 + 1 - z_hi)
    peers_row = [row_device(z_lo, (y * 2 + core + k) % GRID_H, head) for k in range(1, GRID_H)]
    peers_z = [row_device((z_lo + k) % NZ, y * 2 + core, head) for k in range(1, NZ)]
    greet(
        [(d, None) for d in peers_row + peers_z]
        + [(far_half, None), (ring_x(1), None), (ring_x(-1), None), (ring_x(2), None)]
    )
    own_x = pltpu.make_async_copy(x_hbm, xf.at[head], own_s.at[heads])
    own_x.start()
    own_w = []
    for h in range(heads):
        copy = pltpu.make_async_copy(w_hbm.at[:, :, pl.ds(h * HD, HD)], wf.at[h, seq], own_s.at[h])
        copy.start()
        own_w.append(copy)

    def rows_of(ref, which):
        return ref.at[pl.ds(which * piece, piece)]

    def far_copy(which):
        return remote(
            rows_of(x_hbm, which), rows_of(xf.at[head], which), far_s.at[which], far_r.at[which], far_half
        )

    def far_arrival(which):
        ref = rows_of(xf.at[x * 2 + 1 - z_hi], which)
        return remote(ref, ref, far_s.at[which], far_r.at[which], far_half)

    def w_z(h, far_z, direction):
        ref = wf.at[h, seq_of(far_z, y, core)]
        side = 0 if direction > 0 else 1
        return remote(ref, ref, wzs.at[side, far_z, h], wzr.at[far_z, h], line_z(direction))

    def w_y(h, far_z, direction, arriving):
        source = (y - direction + NY) % NY if arriving else y
        ref = wf.at[h, seq_of(far_z, source, core)]
        side = 0 if direction > 0 else 1
        return remote(ref, ref, ys.at[side, far_z, h], yr.at[side, far_z, h], ring_y(direction))

    def w_opposite(h, far_z, direction):
        ref = wf.at[h, seq_of(far_z, (y - direction + NY) % NY, core)]
        return remote(ref, ref, yos.at[far_z, h], yor.at[far_z, h], ring_y(direction))

    def w_core(h, far_z, far_y, order):
        ref = wf.at[h, seq_of(far_z, far_y, core)]
        return remote(ref, ref, cs.at[far_z, order, h], cr.at[far_z, order, h], partner_core)

    def inside(far_z):
        return (far_z >= 0) & (far_z < NZ)

    def have_shard(h, far_z):
        w_y(h, far_z, 1, False).start()
        w_y(h, far_z, -1, False).start()
        w_core(h, far_z, y, 0).start()

    def each_side(step, act):
        if step == 0:
            act(z_lo)
            return
        for direction in (1, -1):
            far_z = z_lo - direction * step

            @pl.when(inside(far_z))
            def _():
                act(far_z)

    def own_shard(h):
        own_w[h].wait()
        for direction in (1, -1):

            @pl.when(inside(z_lo + direction))
            def _():
                w_z(h, z_lo, direction).start()

        have_shard(h, z_lo)

    def z_step(h, step):
        for direction in (1, -1):
            far_z = z_lo - direction * step

            @pl.when(inside(far_z))
            def _():
                w_z(h, far_z, direction).wait_recv()

                @pl.when(inside(z_lo + direction))
                def _():
                    w_z(h, far_z, direction).start()

                have_shard(h, far_z)

    def y_step(h, step):
        def act(far_z):
            for direction in (1, -1):
                w_y(h, far_z, direction, True).wait_recv()

                @pl.when(far_z % 2 == (0 if direction > 0 else 1))
                def _():
                    w_opposite(h, far_z, direction).start()

                w_core(h, far_z, (y - direction + NY) % NY, 1 if direction > 0 else 2).start()

        each_side(step, act)

    def opposite_step(h, step):
        def act(far_z):
            ref = wf.at[h, seq_of(far_z, (y + 2) % NY, core)]
            remote(ref, ref, yos.at[far_z, h], yor.at[far_z, h], ring_y(1)).wait_recv()
            w_core(h, far_z, (y + 2) % NY, 3).start()

        each_side(step, act)

    def core_step(h):
        def act(far_z, _):
            for order in range(4):
                ref = wf.at[h, seq_of(far_z, 0, 1 - core)]
                remote(
                    ref, ref, cs.at[far_z, order, h], cr.at[far_z, order, h], partner_core
                ).wait_recv()
            return 0

        lax.fori_loop(0, NZ, act, 0)

    steps_x = (1, -1, 2)

    def x_near(order, arriving):
        source = x - steps_x[order] if arriving else x
        ref = xf.at[((source + NX) % NX) * 2 + z_hi]
        return remote(ref, ref, xs.at[order], xr.at[order], ring_x(steps_x[order]))

    def x_far(which, order, arriving):
        source = x - steps_x[order] if arriving else x
        ref = rows_of(xf.at[((source + NX) % NX) * 2 + 1 - z_hi], which)
        return remote(ref, ref, ps.at[which, order], pr.at[which, order], ring_x(steps_x[order]))

    def far_step(which):
        far_arrival(which).wait_recv()
        for order in range(3):
            x_far(which, order, False).start()

    peak = jnp.max(hist_ref[...], axis=1, keepdims=True)
    scale_up = LIMIT / peak
    scale_down = peak / LIMIT
    chunks = xf.shape[0]
    width = xf.shape[2]
    features = chunks * width
    block = 16

    def norm_rows(index, largest):
        at = pl.ds(pl.multiple_of(index * block, block), block)
        total = jnp.zeros((block, width), jnp.float32)
        square = jnp.zeros((block, width), jnp.float32)
        for chunk in range(chunks):
            value = xf[chunk, at, :].astype(jnp.float32)
            total = total + value
            square = square + value * value
        mean = jnp.sum(total, axis=1, keepdims=True) * (1.0 / features)
        mean_square = jnp.sum(square, axis=1, keepdims=True) * (1.0 / features)
        inverse = lax.rsqrt(mean_square - mean * mean + EPSILON)
        for chunk in range(chunks):
            value = xf[chunk, at, :].astype(jnp.float32)
            columns = pl.ds(chunk * width, width)
            modulated = (value - mean) * inverse * (1.0 + scale_ref[:, columns]) + shift_ref[:, columns]
            largest = jnp.maximum(largest, jnp.max(jnp.abs(modulated), axis=0, keepdims=True))
            quant[at, columns] = jnp.clip(modulated * scale_up, -LIMIT, LIMIT).astype(jnp.bfloat16)
        return largest

    def norm_step(which):
        for order in range(3):
            x_far(which, order, True).wait_recv()
        per = piece // block
        top[...] = lax.fori_loop(which * per, (which + 1) * per, norm_rows, top[...])

    def near_step():
        for order in range(3):
            x_near(order, True).wait_recv()

    def near_out():
        own_x.wait()
        for order in range(3):
            x_near(order, False).start()

    def project(h):
        depth = wf.shape[1] * wf.shape[3]
        for which in range(3):
            weight = wf[h, :, which].reshape(depth, HD)
            product = jnp.dot(quant[...], weight, preferred_element_type=jnp.float32) * scale_down
            qkv[h, which] = product.astype(jnp.bfloat16).reshape(qkv.shape[2:])

    row = y * 2 + core
    wins = (win0, win1, win2)
    tiles = qkv.shape[2]
    up, down = row_device(z_lo, row - 1, head), row_device(z_lo, row + 1, head)
    before, after = row_device(z_lo - 1, row, head), row_device(z_lo + 1, row, head)
    has_up, has_down = row > 0, row < GRID_H - 1
    has_before, has_after = z_lo > 0, z_lo < NZ - 1
    z_sides = ((0, has_before), (1, has_after))
    row_sides = ((0, has_up), (1, has_down))
    from_rows = ((0, has_down), (1, has_up))
    frames = ((0, has_before), (2, has_after), (1, None))

    def both(p, q):
        return p if q is None else p & q

    def slab(h, slot):
        return wins[h].at[:, pl.ds(slot * tiles, tiles)]

    def z_copy(h, side):
        target, frame = (before, 2) if side == 0 else (after, 0)
        return remote(
            qkv.at[h, pl.ds(1, 2)], slab(h, frame * 3 + 1), zs.at[h, side], zr.at[h, side], target
        )

    def row_copy(h, frame, side):
        target = up if side == 0 else down
        source = qkv.at[h, pl.ds(1, 2)] if frame == 1 else slab(h, frame * 3 + 1)
        return remote(
            source, slab(h, frame * 3 + (2 if side == 0 else 0)),
            rs.at[h, frame, side], rr.at[h, frame, side], target,
        )

    def own_slab(h):
        return pltpu.make_async_copy(qkv.at[h, pl.ds(1, 2)], slab(h, 4), own_s.at[heads + 1 + h])

    def rows_out(h, frame):
        for side, valid in row_sides:

            @pl.when(valid)
            def _():
                row_copy(h, frame, side).start()

    def z_arrive(h):
        for frame, side, valid in ((2, 0, has_after), (0, 1, has_before)):

            @pl.when(valid)
            def _():
                z_copy(h, side).wait_recv()
                rows_out(h, frame)

    def rows_arrive(h):
        for frame, valid_frame in frames:
            for side, valid in from_rows:

                @pl.when(both(valid, valid_frame))
                def _():
                    row_copy(h, frame, side).wait_recv()

        own_slab(h).wait()

    own_peak = pltpu.make_async_copy(peak_own, near.at[row], own_s.at[2 * heads + 1])
    own_far = pltpu.make_async_copy(near, far.at[z_lo], own_s.at[2 * heads + 2])
    def max_near(k):
        return remote(peak_own, near.at[row], ms.at[0, k - 1], mr.at[0, k - 1], peers_row[k - 1])

    def max_far(k):
        return remote(near, far.at[z_lo], ms.at[1, k - 1], mr.at[1, k - 1], peers_z[k - 1])

    def back_row(h, frame, side):
        target = up if side == 0 else down
        return remote(
            parts.at[h, 0 if side == 0 else 2, frame], rows_in.at[h, side, frame],
            bs.at[h, frame, side], br.at[h, frame, side], target,
        )

    def back_z(h, side):
        target = before if side == 0 else after
        return remote(zout.at[h, side], zin.at[h, side], fs.at[h, side], fr.at[h, side], target)

    def back_rows_out(h, frame, valid_frame):
        for side, valid in row_sides:

            @pl.when(both(valid, valid_frame))
            def _():
                back_row(h, frame, side).start()

    def back_rows_arrive(h, frame, valid_frame):
        for side, valid in from_rows:

            @pl.when(both(valid, valid_frame))
            def _():
                back_row(h, frame, side).wait_recv()

    def halo_out(h):
        own_slab(h).start()
        for side, valid in z_sides:

            @pl.when(valid)
            def _():
                z_copy(h, side).start()

        rows_out(h, 1)

    def max_one():
        peak_own[...] = jnp.broadcast_to(jnp.max(top[...], axis=1, keepdims=True), peak_own.shape)

    def max_two():
        own_peak.start()
        for k in range(1, GRID_H):
            max_near(k).start()

    def max_three():
        own_peak.wait()
        for k in range(1, GRID_H):
            max_near(k).wait_recv()
        own_far.start()
        for k in range(1, NZ):
            max_far(k).start()

    def max_four():
        own_far.wait()
        for k in range(1, NZ):
            max_far(k).wait_recv()
        new_hist_ref[0] = jnp.max(far[...])
        for k in range(1, new_hist_ref.shape[0]):
            new_hist_ref[k] = hist_smem[k - 1]

    def prepare():
        def clear(buffer, side):
            for h in range(heads):
                buffer[h, side] = jnp.zeros(buffer.shape[2:], buffer.dtype)

        for side, valid in from_rows:

            @pl.when(jnp.logical_not(valid))
            def _():
                clear(rows_in, side)

        for side, valid in ((0, has_after), (1, has_before)):

            @pl.when(jnp.logical_not(valid))
            def _():
                clear(zin, side)

        for tile in range(tiles):
            gk[tile, KB] = jnp.zeros(gk.shape[2:], gk.dtype)
            gv[tile, KB] = jnp.zeros(gv.shape[2:], gv.dtype)

        for tile in range(tiles):
            for slot in range(KB):
                ids[tile, slot] = 0

        first_slab = (z_lo - 1) * GRID_H + row - 1

        def table(window, _):
            place_slab = first_slab + (window // 9) * GRID_H + (window // 3) % 3
            wanted = place_slab * tiles + window % 3
            for tile in range(tiles):
                found = jnp.int32(KB)
                for slot in range(KB):
                    same = pattern_ref[tile, slot] == wanted
                    found = jnp.where(same, slot, found)
                    ids[tile, slot] = jnp.where(same, window, ids[tile, slot])
                slots[tile, window] = found
            return 0

        def count(slot, _):
            for tile in range(tiles):
                same = [(pattern_ref[tile, slot] == pattern_ref[tile, k]).astype(jnp.int32) for k in range(KB)]
                repeats[tile, slot] = sum(same).astype(jnp.float32)
            return 0

        lax.fori_loop(0, SLOTS * tiles, table, 0)
        lax.fori_loop(0, KB, count, 0)

    def attend(h, tile):
        win = wins[h]
        columns = slice(h * HD, (h + 1) * HD)
        listed = [ids[tile, slot] for slot in range(KB)]
        q = qkv[h, 0, tile]
        g = grad_ref[tile, :, columns]
        keys = jnp.concatenate([win[0, i] for i in listed], axis=0)
        values = jnp.concatenate([win[1, i] for i in listed], axis=0)
        scores = lax.dot_general(
            q, keys, (((1,), (1,)), ((), ())), preferred_element_type=jnp.float32
        )
        top = jnp.max(scores, axis=1, keepdims=True)
        weights = jnp.exp2((scores - top) * EXP2_SCALE)
        prob = weights * (1.0 / jnp.sum(weights, axis=1, keepdims=True))
        low = prob.astype(jnp.bfloat16)
        out = jnp.dot(low, values, preferred_element_type=jnp.float32)
        out_ref[tile, :, columns] = out.astype(jnp.bfloat16)
        gprob = lax.dot_general(
            g, values, (((1,), (1,)), ((), ())), preferred_element_type=jnp.float32
        )
        delta = jnp.sum(g.astype(jnp.float32) * out, axis=1, keepdims=True)
        gscore = (prob * (gprob - delta)).astype(jnp.bfloat16)
        gq = jnp.dot(gscore, keys, preferred_element_type=jnp.float32) * INV_ROOT
        gqkv_ref[0, tile, :, columns] = gq.astype(jnp.bfloat16)
        key_terms = lax.dot_general(
            gscore, q, (((0,), (0,)), ((), ())), preferred_element_type=jnp.float32
        )
        value_terms = lax.dot_general(
            low, g, (((0,), (0,)), ((), ())), preferred_element_type=jnp.float32
        )
        for slot in range(KB):
            span = slice(slot * TILE, (slot + 1) * TILE)
            often = repeats[tile, slot]
            gk[tile, slot] = key_terms[span] * (often * INV_ROOT)
            gv[tile, slot] = value_terms[span] * often
    def give_back(h):
        waiting = None
        for frame, valid_frame in frames:

            def gather(at, _):
                step, column = at // tiles, at % tiles
                window = frame * 9 + at
                found = [slots[tile, window] for tile in range(tiles)]
                key_sum = gk[0, found[0]] + gk[1, found[1]] + gk[2, found[2]]
                value_sum = gv[0, found[0]] + gv[1, found[1]] + gv[2, found[2]]
                parts[h, step, frame, 0, column] = key_sum.astype(jnp.bfloat16)
                parts[h, step, frame, 1, column] = value_sum.astype(jnp.bfloat16)
                return 0

            lax.fori_loop(0, 3 * tiles, gather, 0)
            if waiting is not None:
                back_rows_out(h, *waiting)
            waiting = (frame, valid_frame)
        back_rows_out(h, *waiting)

    def total(h, frame, part, tile):
        return (
            parts[h, 1, frame, part, tile].astype(jnp.float32)
            + rows_in[h, 0, frame, part, tile].astype(jnp.float32)
            + rows_in[h, 1, frame, part, tile].astype(jnp.float32)
        )

    def reduce_rows(h):
        for frame, side, valid_frame in ((0, 0, has_before), (2, 1, has_after)):

            @pl.when(valid_frame)
            def _():
                back_rows_arrive(h, frame, None)

                def add(at, _):
                    part, tile = at // tiles, at % tiles
                    zout[h, side, part, tile] = total(h, frame, part, tile).astype(jnp.bfloat16)
                    return 0

                lax.fori_loop(0, 2 * tiles, add, 0)
                back_z(h, side).start()

    def finish(h):
        back_rows_arrive(h, 1, None)
        for side, valid in ((0, has_after), (1, has_before)):

            @pl.when(valid)
            def _():
                back_z(h, side).wait_recv()

        columns = slice(h * HD, (h + 1) * HD)

        def add(at, _):
            part, tile = at // tiles, at % tiles
            result = (
                total(h, 1, part, tile)
                + zin[h, 0, part, tile].astype(jnp.float32)
                + zin[h, 1, part, tile].astype(jnp.float32)
            )
            gqkv_ref[1 + part, tile, :, columns] = result.astype(jnp.bfloat16)
            return 0

        lax.fori_loop(0, 2 * tiles, add, 0)

    acts = {
        "s": own_shard,
        "z": z_step,
        "y": y_step,
        "o": opposite_step,
        "c": core_step,
        "p": project,
        "x": near_out,
        "a": near_step,
        "i": lambda which: far_copy(which).start(),
        "f": far_step,
        "n": norm_step,
        "h": halo_out,
        "Z": z_arrive,
        "R": rows_arrive,
        "t": attend,
        "g": give_back,
        "r": reduce_rows,
        "F": finish,
        "k": prepare,
        "A": max_one,
        "B": max_two,
        "C": max_three,
        "D": max_four,
    }
    top[...] = jnp.zeros_like(top)
    for item in ORDER:
        acts[item[0]](*[int(digit) for digit in item[1:]])

    for order in range(3):
        x_near(order, False).wait_send()
    for which in range(PIECES):
        far_copy(which).wait_send()
        for order in range(3):
            x_far(which, order, False).wait_send()

    def drain(far_z, _):
        for h in range(heads):
            for direction in (1, -1):
                w_y(h, far_z, direction, False).wait_send()

                @pl.when(inside(z_lo + direction) & ((z_lo - far_z) * direction >= 0))
                def _():
                    w_z(h, far_z, direction).wait_send()

            w_opposite(h, far_z, 1).wait_send()
            for order in range(4):
                w_core(h, far_z, y, order).wait_send()
        return 0

    lax.fori_loop(0, NZ, drain, 0)
    for h in range(heads):
        for side, valid in z_sides:

            @pl.when(valid)
            def _():
                z_copy(h, side).wait_send()
                back_z(h, side).wait_send()

        for frame, valid_frame in frames:
            inward = {0: has_before, 2: has_after, 1: None}[frame]
            for side, valid in row_sides:

                @pl.when(both(valid, inward))
                def _():
                    row_copy(h, frame, side).wait_send()
                    back_row(h, frame, side).wait_send()

    for k in range(1, GRID_H):
        max_near(k).wait_send()
    for k in range(1, NZ):
        max_far(k).wait_send()


def local(block_input, mod_shift, mod_scale, history, w_qkv, pattern, out_cotangent):
    rows, width = block_input.shape
    three, depth, _ = w_qkv.shape
    seqs = lax.axis_size("seq")
    chunks = lax.axis_size("head")
    heads = width // HD
    tiles = rows // TILE
    dma = pltpu.SemaphoreType.DMA
    any_space = pl.BlockSpec(memory_space=pl.ANY)
    vmem = pl.BlockSpec(memory_space=pltpu.VMEM)
    smem = pl.BlockSpec(memory_space=pltpu.SMEM)
    tile = (TILE, HD)
    slab = (2, tiles) + tile
    attn_out, grad_qkv, new_history = pl.pallas_call(
        block_kernel,
        out_shape=(
            jax.ShapeDtypeStruct((tiles, TILE, width), jnp.bfloat16),
            jax.ShapeDtypeStruct((3, tiles, TILE, width), jnp.bfloat16),
            jax.ShapeDtypeStruct(history.shape, jnp.float32),
        ),
        in_specs=[smem, smem, any_space, any_space, vmem, vmem, vmem, vmem],
        out_specs=(vmem, vmem, smem),
        scratch_shapes=[
            pltpu.VMEM((chunks, rows, width), jnp.bfloat16),
            pltpu.VMEM((heads, seqs, three, depth, HD), jnp.bfloat16),
            pltpu.VMEM((rows, chunks * width), jnp.bfloat16),
            pltpu.VMEM((1, width), jnp.float32),
            pltpu.VMEM((8, 128), jnp.float32),
            pltpu.VMEM((heads, 3, tiles) + tile, jnp.bfloat16),
        ]
        + [pltpu.VMEM((2, SLOTS * tiles) + tile, jnp.bfloat16)] * heads
        + [
            pltpu.VMEM((tiles, KB + 1) + tile, jnp.float32),
            pltpu.VMEM((tiles, KB + 1) + tile, jnp.float32),
            pltpu.VMEM((heads, 3, 3) + slab, jnp.bfloat16),
            pltpu.VMEM((heads, 2, 3) + slab, jnp.bfloat16),
            pltpu.VMEM((heads, 2) + slab, jnp.bfloat16),
            pltpu.VMEM((heads, 2) + slab, jnp.bfloat16),
            pltpu.VMEM((GRID_H, 8, 128), jnp.float32),
            pltpu.VMEM((NZ, GRID_H, 8, 128), jnp.float32),
            pltpu.SMEM((tiles, KB), jnp.int32),
            pltpu.SMEM((tiles, SLOTS * tiles), jnp.int32),
            pltpu.SMEM((tiles, KB), jnp.float32),
            dma((2 * heads + 3,)), dma((PIECES,)), dma((PIECES,)),
            dma((3,)), dma((3,)),
            dma((PIECES, 3)), dma((PIECES, 3)),
            dma((2, NZ, heads)), dma((NZ, heads)),
            dma((2, NZ, heads)), dma((2, NZ, heads)),
            dma((NZ, heads)), dma((NZ, heads)),
            dma((NZ, 4, heads)), dma((NZ, 4, heads)),
            dma((heads, 2)), dma((heads, 2)),
            dma((heads, 3, 2)), dma((heads, 3, 2)),
            dma((2, 7)), dma((2, 7)),
            dma((heads, 3, 2)), dma((heads, 3, 2)),
            dma((heads, 2)), dma((heads, 2)),
        ],
        compiler_params=pltpu.CompilerParams(collective_id=0, has_side_effects=True),
        name="block",
    )(
        pattern,
        history,
        block_input,
        w_qkv,
        mod_shift.reshape(1, -1),
        mod_scale.reshape(1, -1),
        history.reshape(1, -1),
        out_cotangent.reshape(tiles, TILE, width),
    )
    return (attn_out.reshape(rows, width), grad_qkv.reshape(3, rows, width), new_history)


def solution(mesh):
    placed = (
        P("seq", "head"),
        P(),
        P(),
        P(),
        P(None, "seq", "head"),
        P("seq", None),
        P("seq", "head"),
    )
    return jax.shard_map(
        local,
        mesh=mesh,
        in_specs=placed,
        out_specs=(P("seq", "head"), P(None, "seq", "head"), P()),
        check_vma=False,
    )
```
